512 devices in a mesh: illum: 32 (over z, y_hi), slab: 8 (over x, core), cuts: 2 (over y_lo).
Axes of the slice: x: 4, y: 8 (y_hi: 4, y_lo: 2; y = y_hi * 2 + y_lo), z: 8, core: 2. Of those that a mesh axis runs over, the one named last changes fastest.
Arguments:
- phase_delay: float32 [4, 256, 1024], P('cuts', 'slab', 'illum'), may hold values from -1.5 to 1.5
- attenuation: float32 [4, 256, 1024], P('cuts', 'slab', 'illum'), may hold values from 0.02 to 0.3
- measured: float32 [32, 2, 256, 1024], P('illum', None, 'slab'), may hold values from -6 to 6
- angles: int32 [32, 2], P('illum'), may hold values from -16 to 16
Outputs:
- grad_phase: float32 [4, 256, 1024], P('cuts', 'slab', 'illum')
- grad_atten: float32 [4, 256, 1024], P('cuts', 'slab', 'illum')
The draws below stay inside these ranges and needn't reach their ends.
All inputs are finite; a program needn't handle non-finite values.
Results may differ from the reference program's by a relative error of at most 0.0001.
Values sent between devices are 32-bit elements; how exact they have to be, the bound alone decides.
No kernel may reach another device: no remote copies, remote signals or barrier semaphores. Data moves between devices by JAX's collectives and lax.ppermute only.
A program may use at most 64 MiB of HBM per device.

```python
import math
import jax
import jax.numpy as jnp

NB = 1024
NA = 256
ILLUMS = 32
NZ = 4


def set_ends(result, key, least, top_value):
    longest = result.shape.index(max(result.shape))
    spots = []
    for shift in (0, 1):
        where = [jax.random.randint(jax.random.fold_in(key, axis), (), 0, length) for axis, length in enumerate(result.shape)]
        where[longest] = (where[longest] + shift) % result.shape[longest]
        spots.append(tuple(where))
    return result.at[spots[0]].set(least).at[spots[1]].set(top_value)


def level_of(rng, extent, shards, low, largest):
    gain, own = 1.0, jax.random.fold_in(rng, 6)
    for dim, blocks in shards:
        draws = jnp.exp(jax.random.uniform(jax.random.fold_in(own, dim), (blocks,), jnp.float32, low / len(shards), largest / len(shards)))
        gain = gain * jnp.repeat(draws, extent[dim] // blocks).reshape([-1 if axis == dim else 1 for axis in range(len(extent))])
    return gain


def normal_values(stream_key, shape, deviation, most, split=(), held_as=jnp.bfloat16):
    drawn = deviation * jax.random.normal(stream_key, shape, jnp.float32)
    if split:
        drawn = drawn * level_of(stream_key, shape, split, -0.22, 0.18)
    return jnp.clip(drawn, -most, most).astype(held_as)


def setup_inputs(seed: int = 0) -> dict:
    seeds = jax.random.split(jax.random.key(seed), 5)
    return {
        "phase_delay": jnp.clip(jax.random.uniform(seeds[0], (NZ, NA, NB), jnp.float32, -1.5, 1.5) * level_of(seeds[0], (NZ, NA, NB), ((0, 2), (1, 8), (2, 32)), -0.4, 0.0), -1.5, 1.5),
        "attenuation": jnp.clip(jnp.exp(math.log(0.3) - 2.7080503 * jax.random.uniform(seeds[1], (NZ, NA, NB), jnp.float32) ** level_of(seeds[1], (NZ, NA, NB), ((0, 2), (1, 8), (2, 32)), -0.2, 0.2)), 0.02, 0.3),
        "measured": normal_values(seeds[2], (ILLUMS, 2, NA, NB), 1.0, 6.0, ((0, 32), (2, 8)), jnp.float32),
        "angles": set_ends(jax.random.randint(seeds[3], (ILLUMS, 2), -16, 17), jax.random.fold_in(seeds[3], 1), -16, 16).astype(jnp.int32),
    }


step_coeff = 0.08
square_coeff = 0.0032


def laplace(values):
    padded = jnp.pad(values, ((0, 0), (0, 0), (1, 1), (1, 1)))
    return (padded[:, :, :-2, 1:-1] + padded[:, :, 2:, 1:-1] + padded[:, :, 1:-1, :-2]
            + padded[:, :, 1:-1, 2:] - 4.0 * values)


def diffract(fields, orient):
    laplace_one = laplace(fields)
    laplace_two = laplace(laplace_one)
    real_part = fields[:, 0] - orient * step_coeff * laplace_one[:, 1] - square_coeff * laplace_two[:, 0]
    imag_part = fields[:, 1] + orient * step_coeff * laplace_one[:, 0] - square_coeff * laplace_two[:, 1]
    return jnp.stack((real_part, imag_part), axis=1)


def incident_wave(angles, row_ids, total_rows, total_cols):
    column_ids = jnp.arange(total_cols, dtype=jnp.int32)
    row_turns = angles[:, 0].astype(jnp.int32)[:, None, None]
    col_turns = angles[:, 1].astype(jnp.int32)[:, None, None]
    fraction = (jnp.mod(row_turns * row_ids[None, :, None], total_rows).astype(jnp.float32) / total_rows
                + jnp.mod(col_turns * column_ids[None, None, :], total_cols).astype(jnp.float32) / total_cols)
    phase_angle = 2.0 * math.pi * fraction
    return jnp.stack((jnp.cos(phase_angle), jnp.sin(phase_angle)), axis=1)


def complex_times(pair, fields):
    trans_real, trans_imag = pair
    return jnp.stack((trans_real * fields[:, 0] - trans_imag * fields[:, 1],
                      trans_real * fields[:, 1] + trans_imag * fields[:, 0]), axis=1)


def conj_times(pair, fields):
    trans_real, trans_imag = pair
    return jnp.stack((trans_real * fields[:, 0] + trans_imag * fields[:, 1],
                      trans_real * fields[:, 1] - trans_imag * fields[:, 0]), axis=1)


def reference(phase_delay, attenuation, measured, angles):
    fields = incident_wave(angles, jnp.arange(NA, dtype=jnp.int32), NA, NB)
    transmit = []
    stored = []
    for layer_index in range(NZ):
        damping = jnp.exp(-attenuation[layer_index])
        pair = (damping * jnp.cos(phase_delay[layer_index]), damping * jnp.sin(phase_delay[layer_index]))
        transmit.append(pair)
        passed = complex_times(pair, fields)
        stored.append(passed)
        fields = diffract(passed, 1.0)
    adjoint = fields - measured
    phase_list = [None] * NZ
    atten_list = [None] * NZ
    for layer_index in reversed(range(NZ)):
        weighted = diffract(adjoint, -1.0)
        passed = stored[layer_index]
        phase_list[layer_index] = -jnp.sum(passed[:, 1] * weighted[:, 0] - passed[:, 0] * weighted[:, 1], axis=0)
        atten_list[layer_index] = -jnp.sum(passed[:, 0] * weighted[:, 0] + passed[:, 1] * weighted[:, 1], axis=0)
        adjoint = conj_times(transmit[layer_index], weighted)
    return jnp.stack(phase_list), jnp.stack(atten_list)
```

```python
import functools
import math

import jax
import jax.numpy as jnp
from jax import lax
from jax.experimental import pallas as pl
from jax.experimental.pallas import tpu as pltpu
from jax.sharding import PartitionSpec as P

step_coeff = 0.08
square_coeff = 0.0032
ratio = step_coeff / square_coeff
two_pi = 2.0 * math.pi

HALO = 8
REACH = 16
VMEM = pl.BlockSpec(memory_space=pltpu.VMEM)
SMEM = pl.BlockSpec(memory_space=pltpu.SMEM)
small = pltpu.CompilerParams(vmem_limit_bytes=1 << 20)
large = pltpu.CompilerParams(vmem_limit_bytes=8 << 20)


def f32(*shape):
    return jax.ShapeDtypeStruct(shape, jnp.float32)


def lanes_of(shape):
    return lax.broadcasted_iota(jnp.int32, shape, 1)


def turn(x, by):
    by %= 128
    return pltpu.roll(x, by, 1) if by else x


def pack_object(phase_ref, atten_ref, out_ref):
    for n, (ref, layer) in enumerate(
        ((phase_ref, 0), (phase_ref, 1), (atten_ref, 0), (atten_ref, 1))
    ):
        out_ref[:, 32 * n : 32 * n + 32] = ref[layer]


def pack_edges(ids_ref, mine_ref, other_ref, out_ref):
    first = ids_ref[2] == 0
    for pair, (a, b) in enumerate(((mine_ref, other_ref), (other_ref, mine_ref))):
        out_ref[pair] = jnp.where(
            first, jnp.where(first, a[0:8], b[0:8]), jnp.where(first, a[24:32], b[24:32])
        )


def pack_rows(ids_ref, mine_ref, other_ref, edge_ref, out_ref):
    first = ids_ref[2] == 0
    for pair in range(2):
        for block in range(4):
            rows = slice(8 * block, 8 * block + 8)
            above = edge_ref[pair] if block == 0 else None
            below = edge_ref[pair] if block == 3 else None
            refs = (mine_ref, other_ref) if pair == 0 else (other_ref, mine_ref)
            if above is None:
                above = refs[0][8 * block - 8 : 8 * block]
            if below is None:
                below = refs[1][8 * block + 8 : 8 * block + 16]
            out_ref[pair, rows] = jnp.where(first, above, below)


def pack_measured(ids_ref, angles_ref, measured_ref, out_ref):
    lane = lanes_of((8, 128))
    row = lax.broadcasted_iota(jnp.int32, (8, 128), 0)
    turns = [angles_ref[0, k].astype(jnp.float32) for k in range(2)]
    zero = jnp.zeros((8, 128), jnp.float32)
    for comp in range(2):
        halves = []
        for a in range(2):
            full = measured_ref[0, comp, 8 * a : 8 * a + 8, :]
            halves.append([full[:, 128 * n : 128 * n + 128] for n in range(8)])
        for j in range(32):
            v, r = divmod(32 * j - REACH, 128)
            parts = []
            for a in range(2):
                regs = halves[a]
                left = regs[v] if v >= 0 else zero
                part = turn(left, 64 * a - r)
                if r > 64:
                    right = regs[v + 1] if v + 1 < 8 else zero
                    part = jnp.where(lane - 64 * a < 128 - r, part, turn(right, 64 * a - r))
                parts.append(part)
            both = jnp.where(lane < 64, parts[0], parts[1])
            if comp == 0:
                both = jnp.where(lane == 0, turns[0], jnp.where(lane == 1, turns[1], both))
            out_ref[j, 8 * comp : 8 * comp + 8] = both


def side_sum(x):
    return turn(x, 1) + turn(x, 127)


def march(
    ids_ref, here_ref, left_ref, right_ref, got_ref,
    mine_ref, other_ref, across_ref, along_ref,
    plain, table, field, stored, acc, low, high,
):
    block, slab, cut = ids_ref[0], ids_ref[1], ids_ref[2]
    first = cut == 0
    lane = lanes_of((8, 128))
    sub = lax.broadcasted_iota(jnp.int32, (8, 128), 0)
    window = jnp.bitwise_and(lane, 63)
    upper = lane < 64
    column = 32 * block - REACH + window
    top = 32 * slab + 16 * cut - HALO
    column_inside = (column >= 0) & (column < 1024)

    for q in range(2):
        row = top + sub + 8 * q + jnp.where(upper, 0, 16)
        inside = column_inside & (row >= 0) & (row < 256)
        plain[8, 8 * q : 8 * q + 8] = jnp.where(inside, square_coeff, 0.0)
        for layer in range(4):
            pair, sl = divmod(layer, 2)
            values = []
            for n in (sl, 2 + sl):
                halves = []
                for a in range(2):
                    rows = slice(16 * a + 8 * q, 16 * a + 8 * q + 8)
                    at = 64 * a - 32 * n
                    halves.append(
                        jnp.where(
                            window < 16,
                            turn(left_ref[pair, rows], at - 16),
                            jnp.where(
                                window < 48,
                                turn(here_ref[pair, rows], at + 16),
                                turn(right_ref[pair, rows], at + 48),
                            ),
                        )
                    )
                values.append(jnp.where(upper, halves[0], halves[1]))
            damping = jnp.where(inside, jnp.exp(-values[1]), 0.0)
            plain[2 * layer, 8 * q : 8 * q + 8] = damping * jnp.cos(values[0])
            plain[2 * layer + 1, 8 * q : 8 * q + 8] = damping * jnp.sin(values[0])
    upper_row = lanes_of((1, 128)) < 64
    for n in range(9):
        for r in range(16):
            table[n, r : r + 1] = jnp.where(
                upper_row, plain[n, r : r + 1], plain[n, 15 - r : 16 - r]
            )
    acc[...] = jnp.zeros_like(acc)
    column_mask = jnp.where(column_inside, 1.0, 0.0)

    def spread(n, r):
        return jnp.broadcast_to(table[n, r : r + 1], (8, 128))

    def diffract(source, begin, inner, orient, emit):
        rows, scaled = {}, {}

        def around(values, r, k):
            parts = [values[n][k] for n in (r - 1, r + 1) if n in values]
            if r in values:
                parts.append(side_sum(values[r][k]))
            return functools.reduce(lambda x, y: x + y, parts)

        def scale(r):
            mask = spread(8, r)
            out = []
            for k in range(2):
                total = around(rows, r, k)
                if r in rows:
                    total = total - 4.0 * rows[r][k]
                out.append(mask * total)
            scaled[r] = tuple(out)

        def finish(r):
            re, im = (-around(scaled, r, k) for k in range(2))
            if r in rows:
                re, im = re + rows[r][0], im + rows[r][1]
            if r in scaled:
                mre, mim = scaled[r]
                turned = orient * ratio
                re = re + (4.0 * mre - turned * mim)
                im = im + (4.0 * mim + turned * mre)
            emit(r, re, im)

        def advance(r):
            if r - 1 >= begin + inner:
                scale(r - 1)
            if r - 2 >= begin + 2 * inner:
                finish(r - 2)

        for r in range(begin, 16):
            rows[r] = source(r)
            advance(r)
        rows[16] = tuple(turn(x, 64) for x in rows[15])
        advance(16)
        scaled[16] = tuple(turn(x, 64) for x in scaled[15])
        finish(15)

    @pl.loop(0, 4)
    def _(group):
        start = group * 128

        def received(comp, k):
            return got_ref[pl.ds(start + 8 * comp + k, 8, stride=16), :]

        head = received(0, 0)
        row_turns = jnp.broadcast_to(head[:, 0:1], (8, 128))
        col_turns = jnp.broadcast_to(head[:, 1:2], (8, 128))
        row0 = (top + jnp.where(upper, 0, 31)).astype(jnp.float32)
        row_part = row_turns * row0 * (1.0 / 256.0)
        col_part = col_turns * column.astype(jnp.float32) * (1.0 / 1024.0)
        row_part = row_part - jnp.floor(row_part)
        col_part = col_part - jnp.floor(col_part)
        t = two_pi * (row_part + col_part)
        wave = [(jnp.cos(t), jnp.sin(t))]
        t = two_pi / 256.0 * row_turns * jnp.where(upper, 1.0, -1.0)
        step = (jnp.cos(t), jnp.sin(t))

        def from_wave(r):
            re, im = wave[-1]
            wave.append((re * step[0] - im * step[1], re * step[1] + im * step[0]))
            return (re, im)

        def from_field(r):
            return (field[0, r], field[1, r])

        def forward(layer):
            def source(r):
                re, im = from_wave(r) if layer == 0 else from_field(r)
                a, b = spread(2 * layer, r), spread(2 * layer + 1, r)
                v = (a * re - b * im, a * im + b * re)
                stored[2 * layer, r], stored[2 * layer + 1, r] = v
                return v

            def emit(r, re, im):
                if layer == 3:
                    k = r - 8
                    field[0, r] = column_mask * (
                        re - jnp.where(upper, received(0, k), received(0, 7 - k))
                    )
                    field[1, r] = column_mask * (
                        im - jnp.where(upper, received(1, k), received(1, 7 - k))
                    )
                else:
                    field[0, r], field[1, r] = re, im

            diffract(source, 2 * layer, 1, 1.0, emit)

        def backward(layer):
            def emit(r, re, im):
                vre, vim = stored[2 * layer, r], stored[2 * layer + 1, r]
                acc[2 * layer, r] += vre * im - vim * re
                acc[2 * layer + 1, r] -= vre * re + vim * im
                if layer:
                    a, b = spread(2 * layer, r), spread(2 * layer + 1, r)
                    field[0, r], field[1, r] = a * re + b * im, a * im - b * re

            diffract(from_field, 2 * layer + 2, -1, -1.0, emit)

        for layer in range(4):
            forward(layer)
        for layer in (3, 2, 1, 0):
            backward(layer)

    for n in range(8):
        for r in range(16):
            row = jnp.sum(acc[n, r], axis=0, keepdims=True)
            low[n, r : r + 1] = row
            high[n, 15 - r : 16 - r] = row
    blocks = []
    for pair in range(2):
        parts = []
        for b in range(4):
            ref, shift = (low, 16) if b < 2 else (high, 80)
            rows = slice(8 * (b % 2), 8 * (b % 2) + 8)
            total = None
            for n in range(4):
                out, sl = divmod(n, 2)
                x = turn(ref[2 * (2 * pair + sl) + out, rows], 32 * n - shift)
                total = x if total is None else jnp.where(lane < 32 * n, total, x)
            parts.append(total)
        blocks.append(parts)
    mine = [jnp.where(first, a, b) for a, b in zip(*blocks)]
    other = [jnp.where(first, b, a) for a, b in zip(*blocks)]
    none = jnp.zeros((8, 128), jnp.float32)
    for parts, ref in ((mine, mine_ref), (other, other_ref)):
        for b in range(4):
            ref[8 * b : 8 * b + 8] = jnp.where(
                first, parts[b + 1] if b < 3 else none, parts[b - 1] if b > 0 else none
            )
    across_ref[...] = jnp.where(first, other[0], other[3])
    along_ref[...] = jnp.where(first, mine[0], mine[3])


def combine(ids_ref, mine_ref, other_ref, across_ref, along_ref, phase_ref, atten_ref):
    first = ids_ref[2] == 0
    for b in range(4):
        rows = slice(8 * b, 8 * b + 8)
        total = mine_ref[rows] + other_ref[rows]
        if b == 0:
            total = total + jnp.where(first, across_ref[...], along_ref[...])
        if b == 3:
            total = total + jnp.where(first, along_ref[...], across_ref[...])
        for sl in range(2):
            phase_ref[sl, rows] = turn(total, -32 * sl)[:, 0:32]
            atten_ref[sl, rows] = turn(total, -64 - 32 * sl)[:, 0:32]


def body(phase_delay, attenuation, measured, angles):
    block = lax.axis_index("illum")
    slab = lax.axis_index("slab")
    cut = lax.axis_index("cuts")
    ids = jnp.stack([block, slab, cut]).astype(jnp.int32)
    n_slabs, n_blocks = lax.axis_size("slab"), lax.axis_size("illum")
    rows_axis = ("slab", "cuts")

    def both_ways(pairs):
        return pairs + [(b, a) for a, b in pairs]

    partner = both_ways([(2 * s, 2 * s + 1) for s in range(n_slabs)])
    across = both_ways([(2 * s + 1, 2 * s + 2) for s in range(n_slabs - 1)])
    along = [(2 * s + 1, 2 * s + 3) for s in range(n_slabs - 1)]
    along += [(2 * s + 2, 2 * s) for s in range(n_slabs - 1)]

    mine = pl.pallas_call(
        pack_object,
        out_shape=f32(32, 128),
        in_specs=[VMEM, VMEM],
        out_specs=VMEM,
        compiler_params=small,
    )(phase_delay, attenuation)
    other = lax.ppermute(mine, rows_axis, partner)
    edges = pl.pallas_call(
        pack_edges,
        out_shape=f32(2, 8, 128),
        in_specs=[SMEM, VMEM, VMEM],
        out_specs=VMEM,
        compiler_params=small,
    )(ids, mine, other)
    edges = lax.ppermute(edges, rows_axis, across)
    here = pl.pallas_call(
        pack_rows,
        out_shape=f32(2, 32, 128),
        in_specs=[SMEM] + [VMEM] * 3,
        out_specs=VMEM,
        compiler_params=small,
    )(ids, mine, other, edges)
    from_left = lax.ppermute(here, "illum", [(i, i + 1) for i in range(n_blocks - 1)])
    from_right = lax.ppermute(here, "illum", [(i + 1, i) for i in range(n_blocks - 1)])

    sent = pl.pallas_call(
        pack_measured,
        out_shape=f32(32, 16, 128),
        grid_spec=pltpu.PrefetchScalarGridSpec(
            num_scalar_prefetch=1,
            grid=(1,),
            in_specs=[
                SMEM,
                pl.BlockSpec((1, 2, 16, 1024), lambda g, ids: (0, 0, ids[2], 0)),
            ],
            out_specs=pl.BlockSpec((32, 16, 128), lambda g, ids: (0, 0, 0)),
        ),
        compiler_params=large,
    )(ids, angles, measured)
    got = lax.all_to_all(sent, "illum", 0, 0, tiled=True)

    mine, other, across_part, along_part = pl.pallas_call(
        march,
        out_shape=(f32(32, 128), f32(32, 128), f32(8, 128), f32(8, 128)),
        in_specs=[SMEM] + [VMEM] * 4,
        out_specs=(VMEM,) * 4,
        scratch_shapes=[
            pltpu.VMEM((9, 16, 128), jnp.float32),
            pltpu.VMEM((9, 16, 128), jnp.float32),
            pltpu.VMEM((2, 16, 8, 128), jnp.float32),
            pltpu.VMEM((8, 16, 8, 128), jnp.float32),
            pltpu.VMEM((8, 16, 8, 128), jnp.float32),
            pltpu.VMEM((8, 16, 128), jnp.float32),
            pltpu.VMEM((8, 16, 128), jnp.float32),
        ],
        compiler_params=large,
    )(ids, here, from_left, from_right, got.reshape(512, 128))
    other = lax.ppermute(other, rows_axis, partner)
    across_part = lax.ppermute(across_part, rows_axis, across)
    along_part = lax.ppermute(along_part, rows_axis, along)
    return pl.pallas_call(
        combine,
        out_shape=(f32(2, 32, 32), f32(2, 32, 32)),
        in_specs=[SMEM] + [VMEM] * 4,
        out_specs=(VMEM, VMEM),
        compiler_params=small,
    )(ids, mine, other, across_part, along_part)


def solution(mesh):
    placed = (
        P("cuts", "slab", "illum"),
        P("cuts", "slab", "illum"),
        P("illum", None, "slab", None),
        P("illum", None),
    )
    return jax.shard_map(
        body,
        mesh=mesh,
        in_specs=placed,
        out_specs=(P("cuts", "slab", "illum"), P("cuts", "slab", "illum")),
        check_vma=False,
    )
```

```python
import functools
import math

import jax
import jax.numpy as jnp
from jax import lax
from jax.experimental import pallas as pl
from jax.experimental.pallas import tpu as pltpu
from jax.sharding import PartitionSpec as P


step_coeff = 0.08
square_coeff = 0.0032
ratio = step_coeff / square_coeff
two_pi = 2.0 * math.pi

HALO = 8
REACH = 16
VMEM = pl.BlockSpec(memory_space=pltpu.VMEM)
SMEM = pl.BlockSpec(memory_space=pltpu.SMEM)
HBM = pl.BlockSpec(memory_space=pltpu.HBM)
small = pltpu.CompilerParams(vmem_limit_bytes=1 << 20)
large = pltpu.CompilerParams(vmem_limit_bytes=8 << 20)


def f32(*shape):
    return jax.ShapeDtypeStruct(shape, jnp.float32)


def lanes_of(shape):
    return lax.broadcasted_iota(jnp.int32, shape, 1)


def turn(x, by):
    by %= 128
    return pltpu.roll(x, by, 1) if by else x


def pack_object(
    ids_ref, phase_ref, atten_ref, measured_ref, angles_ref,
    out_ref, half_ref, head_ref,
    phase, atten, turns, sems,
):
    copies = [
        pltpu.make_async_copy(phase_ref, phase, sems.at[0]),
        pltpu.make_async_copy(atten_ref, atten, sems.at[1]),
        pltpu.make_async_copy(angles_ref, turns, sems.at[2]),
        pltpu.make_async_copy(
            measured_ref.at[0, :, pl.ds(pl.multiple_of(16 * ids_ref[2], 16), 16), :],
            half_ref,
            sems.at[3],
        ),
    ]
    for copy in copies:
        copy.start()
    for copy in copies[:3]:
        copy.wait()
    for n, (ref, layer) in enumerate(((phase, 0), (phase, 1), (atten, 0), (atten, 1))):
        out_ref[:, 32 * n : 32 * n + 32] = ref[layer]
    lane = lanes_of((8, 128))
    head_ref[...] = jnp.where(lane == 0, turns[0, 0], turns[0, 1]).astype(jnp.float32)
    copies[3].wait()


def pack_edges(ids_ref, mine_ref, other_ref, out_ref):
    first = ids_ref[2] == 0
    for pair, (a, b) in enumerate(((mine_ref, other_ref), (other_ref, mine_ref))):
        out_ref[pair] = jnp.where(
            first, jnp.where(first, a[0:8], b[0:8]), jnp.where(first, a[24:32], b[24:32])
        )


def pack_rows(ids_ref, mine_ref, other_ref, edge_ref, out_ref):
    first = ids_ref[2] == 0
    for pair in range(2):
        for block in range(4):
            rows = slice(8 * block, 8 * block + 8)
            above = edge_ref[pair] if block == 0 else None
            below = edge_ref[pair] if block == 3 else None
            refs = (mine_ref, other_ref) if pair == 0 else (other_ref, mine_ref)
            if above is None:
                above = refs[0][8 * block - 8 : 8 * block]
            if below is None:
                below = refs[1][8 * block + 8 : 8 * block + 16]
            out_ref[pair, rows] = jnp.where(first, above, below)


def pack_measured(half_ref, head_ref, out_ref, packed, sems):
    lane = lanes_of((8, 128))
    zero = jnp.zeros((8, 128), jnp.float32)
    regs = [
        [
            [half_ref[comp, 8 * a : 8 * a + 8, 128 * n : 128 * n + 128] for n in range(8)]
            for a in range(2)
        ]
        for comp in range(2)
    ]
    copies = []
    for j in range(32):
        v, r = divmod(32 * j - REACH, 128)
        for comp in range(2):
            parts = []
            for a in range(2):
                left = regs[comp][a][v] if v >= 0 else zero
                part = turn(left, 64 * a - r)
                if r > 64:
                    right = regs[comp][a][v + 1] if v + 1 < 8 else zero
                    part = jnp.where(lane - 64 * a < 128 - r, part, turn(right, 64 * a - r))
                parts.append(part)
            both = jnp.where(lane < 64, parts[0], parts[1])
            if comp == 0:
                both = jnp.where(lane < 2, head_ref[...], both)
            packed[j, 8 * comp : 8 * comp + 8] = both
        if j % 8 == 7:
            part = pl.ds(j - 7, 8)
            copies.append(
                pltpu.make_async_copy(packed.at[part], out_ref.at[part], sems.at[j // 8])
            )
            copies[-1].start()
    for copy in copies:
        copy.wait()


def side_sum(x):
    return turn(x, 1) + turn(x, 127)


def march(
    ids_ref, here_ref, left_ref, right_ref, got_ref,
    mine_ref, other_ref, across_ref, along_ref,
    plain, table, field, stored, acc, low, high,
):
    block, slab, cut = ids_ref[0], ids_ref[1], ids_ref[2]
    first = cut == 0
    lane = lanes_of((8, 128))
    sub = lax.broadcasted_iota(jnp.int32, (8, 128), 0)
    window = jnp.bitwise_and(lane, 63)
    upper = lane < 64
    column = 32 * block - REACH + window
    top = 32 * slab + 16 * cut - HALO
    column_inside = (column >= 0) & (column < 1024)

    for q in range(2):
        row = top + sub + 8 * q + jnp.where(upper, 0, 16)
        inside = column_inside & (row >= 0) & (row < 256)
        plain[8, 8 * q : 8 * q + 8] = jnp.where(inside, square_coeff, 0.0)
        for layer in range(4):
            pair, sl = divmod(layer, 2)
            values = []
            for n in (sl, 2 + sl):
                halves = []
                for a in range(2):
                    rows = slice(16 * a + 8 * q, 16 * a + 8 * q + 8)
                    at = 64 * a - 32 * n
                    halves.append(
                        jnp.where(
                            window < 16,
                            turn(left_ref[pair, rows], at - 16),
                            jnp.where(
                                window < 48,
                                turn(here_ref[pair, rows], at + 16),
                                turn(right_ref[pair, rows], at + 48),
                            ),
                        )
                    )
                values.append(jnp.where(upper, halves[0], halves[1]))
            damping = jnp.where(inside, jnp.exp(-values[1]), 0.0)
            plain[2 * layer, 8 * q : 8 * q + 8] = damping * jnp.cos(values[0])
            plain[2 * layer + 1, 8 * q : 8 * q + 8] = damping * jnp.sin(values[0])
    upper_row = lanes_of((1, 128)) < 64
    for n in range(9):
        for r in range(16):
            table[n, r : r + 1] = jnp.where(
                upper_row, plain[n, r : r + 1], plain[n, 15 - r : 16 - r]
            )
    acc[...] = jnp.zeros_like(acc)
    column_mask = jnp.where(column_inside, 1.0, 0.0)

    def spread(n, r):
        return jnp.broadcast_to(table[n, r : r + 1], (8, 128))

    def diffract(source, begin, inner, orient, emit):
        rows, scaled = {}, {}

        def around(values, r, k):
            parts = [values[n][k] for n in (r - 1, r + 1) if n in values]
            if r in values:
                parts.append(side_sum(values[r][k]))
            return functools.reduce(lambda x, y: x + y, parts)

        def scale(r):
            mask = spread(8, r)
            out = []
            for k in range(2):
                total = around(rows, r, k)
                if r in rows:
                    total = total - 4.0 * rows[r][k]
                out.append(mask * total)
            scaled[r] = tuple(out)

        def finish(r):
            re, im = (-around(scaled, r, k) for k in range(2))
            if r in rows:
                re, im = re + rows[r][0], im + rows[r][1]
            if r in scaled:
                mre, mim = scaled[r]
                turned = orient * ratio
                re = re + (4.0 * mre - turned * mim)
                im = im + (4.0 * mim + turned * mre)
            emit(r, re, im)

        def advance(r):
            if r - 1 >= begin + inner:
                scale(r - 1)
            if r - 2 >= begin + 2 * inner:
                finish(r - 2)

        for r in range(begin, 16):
            rows[r] = source(r)
            advance(r)
        rows[16] = tuple(turn(x, 64) for x in rows[15])
        advance(16)
        scaled[16] = tuple(turn(x, 64) for x in scaled[15])
        finish(15)

    @pl.loop(0, 4)
    def _(group):
        start = group * 128

        def received(comp, k):
            return got_ref[pl.ds(start + 8 * comp + k, 8, stride=16), :]

        head = received(0, 0)
        row_turns = jnp.broadcast_to(head[:, 0:1], (8, 128))
        col_turns = jnp.broadcast_to(head[:, 1:2], (8, 128))
        row0 = (top + jnp.where(upper, 0, 31)).astype(jnp.float32)
        row_part = row_turns * row0 * (1.0 / 256.0)
        col_part = col_turns * column.astype(jnp.float32) * (1.0 / 1024.0)
        row_part = row_part - jnp.floor(row_part)
        col_part = col_part - jnp.floor(col_part)
        t = two_pi * (row_part + col_part)
        wave = [(jnp.cos(t), jnp.sin(t))]
        t = two_pi / 256.0 * row_turns * jnp.where(upper, 1.0, -1.0)
        step = (jnp.cos(t), jnp.sin(t))

        def from_wave():
            re, im = wave[-1]
            wave.append((re * step[0] - im * step[1], re * step[1] + im * step[0]))
            return (re, im)

        def from_field(r):
            return (field[0, r], field[1, r])

        def forward(layer):
            def source(r):
                re, im = from_wave() if layer == 0 else from_field(r)
                a, b = spread(2 * layer, r), spread(2 * layer + 1, r)
                v = (a * re - b * im, a * im + b * re)
                stored[2 * layer, r], stored[2 * layer + 1, r] = v
                return v

            def emit(r, re, im):
                if layer == 3:
                    k = r - 8
                    field[0, r] = column_mask * (
                        re - jnp.where(upper, received(0, k), received(0, 7 - k))
                    )
                    field[1, r] = column_mask * (
                        im - jnp.where(upper, received(1, k), received(1, 7 - k))
                    )
                else:
                    field[0, r], field[1, r] = re, im

            diffract(source, 2 * layer, 1, 1.0, emit)

        def backward(layer):
            def emit(r, re, im):
                vre, vim = stored[2 * layer, r], stored[2 * layer + 1, r]
                acc[2 * layer, r] += vre * im - vim * re
                acc[2 * layer + 1, r] -= vre * re + vim * im
                if layer:
                    a, b = spread(2 * layer, r), spread(2 * layer + 1, r)
                    field[0, r], field[1, r] = a * re + b * im, a * im - b * re

            diffract(from_field, 2 * layer + 2, -1, -1.0, emit)

        for layer in range(4):
            forward(layer)
        for layer in (3, 2, 1, 0):
            backward(layer)

    for n in range(8):
        for r in range(16):
            row = jnp.sum(acc[n, r], axis=0, keepdims=True)
            low[n, r : r + 1] = row
            high[n, 15 - r : 16 - r] = row
    blocks = []
    for pair in range(2):
        parts = []
        for b in range(4):
            ref, shift = (low, 16) if b < 2 else (high, 80)
            rows = slice(8 * (b % 2), 8 * (b % 2) + 8)
            total = None
            for n in range(4):
                out, sl = divmod(n, 2)
                x = turn(ref[2 * (2 * pair + sl) + out, rows], 32 * n - shift)
                total = x if total is None else jnp.where(lane < 32 * n, total, x)
            parts.append(total)
        blocks.append(parts)
    mine = [jnp.where(first, a, b) for a, b in zip(*blocks)]
    other = [jnp.where(first, b, a) for a, b in zip(*blocks)]
    none = jnp.zeros((8, 128), jnp.float32)
    for parts, ref in ((mine, mine_ref), (other, other_ref)):
        for b in range(4):
            ref[8 * b : 8 * b + 8] = jnp.where(
                first, parts[b + 1] if b < 3 else none, parts[b - 1] if b > 0 else none
            )
    across_ref[...] = jnp.where(first, other[0], other[3])
    along_ref[...] = jnp.where(first, mine[0], mine[3])


def combine(ids_ref, mine_ref, other_ref, across_ref, along_ref, phase_ref, atten_ref):
    first = ids_ref[2] == 0
    for b in range(4):
        rows = slice(8 * b, 8 * b + 8)
        total = mine_ref[rows] + other_ref[rows]
        if b == 0:
            total = total + jnp.where(first, across_ref[...], along_ref[...])
        if b == 3:
            total = total + jnp.where(first, along_ref[...], across_ref[...])
        for sl in range(2):
            phase_ref[sl, rows] = turn(total, -32 * sl)[:, 0:32]
            atten_ref[sl, rows] = turn(total, -64 - 32 * sl)[:, 0:32]


def body(phase_delay, attenuation, measured, angles):
    block = lax.axis_index("illum")
    slab = lax.axis_index("slab")
    cut = lax.axis_index("cuts")
    ids = jnp.stack([block, slab, cut]).astype(jnp.int32)
    n_slabs, n_blocks = lax.axis_size("slab"), lax.axis_size("illum")
    rows_axis = ("slab", "cuts")

    def both_ways(pairs):
        return pairs + [(b, a) for a, b in pairs]

    partner = both_ways([(2 * s, 2 * s + 1) for s in range(n_slabs)])
    across = both_ways([(2 * s + 1, 2 * s + 2) for s in range(n_slabs - 1)])
    along = [(2 * s + 1, 2 * s + 3) for s in range(n_slabs - 1)]
    along += [(2 * s + 2, 2 * s) for s in range(n_slabs - 1)]

    mine, half, head = pl.pallas_call(
        pack_object,
        out_shape=(f32(32, 128), f32(2, 16, 1024), f32(8, 128)),
        in_specs=[SMEM] + [HBM] * 4,
        out_specs=(VMEM,) * 3,
        scratch_shapes=[
            pltpu.VMEM((2, 32, 32), jnp.float32),
            pltpu.VMEM((2, 32, 32), jnp.float32),
            pltpu.SMEM((1, 2), jnp.int32),
            pltpu.SemaphoreType.DMA((4,)),
        ],
        compiler_params=small,
    )(
        ids,
        *(
            pltpu.with_memory_space_constraint(x, pltpu.HBM)
            for x in (phase_delay, attenuation, measured, angles)
        ),
    )
    other = lax.ppermute(mine, rows_axis, partner)
    sent = pl.pallas_call(
        pack_measured,
        out_shape=f32(32, 16, 128),
        in_specs=[VMEM, VMEM],
        out_specs=HBM,
        scratch_shapes=[
            pltpu.VMEM((32, 16, 128), jnp.float32),
            pltpu.SemaphoreType.DMA((4,)),
        ],
        compiler_params=small,
    )(half, head)
    edges = pl.pallas_call(
        pack_edges,
        out_shape=f32(2, 8, 128),
        in_specs=[SMEM, VMEM, VMEM],
        out_specs=VMEM,
        compiler_params=small,
    )(ids, mine, other)
    edges = lax.ppermute(edges, rows_axis, across)
    got = lax.all_to_all(sent, "illum", 0, 0, tiled=True)
    here = pl.pallas_call(
        pack_rows,
        out_shape=f32(2, 32, 128),
        in_specs=[SMEM] + [VMEM] * 3,
        out_specs=VMEM,
        compiler_params=small,
    )(ids, mine, other, edges)
    from_left = lax.ppermute(here, "illum", [(i, i + 1) for i in range(n_blocks - 1)])
    from_right = lax.ppermute(here, "illum", [(i + 1, i) for i in range(n_blocks - 1)])

    mine, other, across_part, along_part = pl.pallas_call(
        march,
        out_shape=(f32(32, 128), f32(32, 128), f32(8, 128), f32(8, 128)),
        in_specs=[SMEM] + [VMEM] * 4,
        out_specs=(VMEM,) * 4,
        scratch_shapes=[
            pltpu.VMEM((9, 16, 128), jnp.float32),
            pltpu.VMEM((9, 16, 128), jnp.float32),
            pltpu.VMEM((2, 16, 8, 128), jnp.float32),
            pltpu.VMEM((8, 16, 8, 128), jnp.float32),
            pltpu.VMEM((8, 16, 8, 128), jnp.float32),
            pltpu.VMEM((8, 16, 128), jnp.float32),
            pltpu.VMEM((8, 16, 128), jnp.float32),
        ],
        compiler_params=large,
    )(ids, here, from_left, from_right, got.reshape(512, 128))
    other = lax.ppermute(other, rows_axis, partner)
    across_part = lax.ppermute(across_part, rows_axis, across)
    along_part = lax.ppermute(along_part, rows_axis, along)
    return pl.pallas_call(
        combine,
        out_shape=(f32(2, 32, 32), f32(2, 32, 32)),
        in_specs=[SMEM] + [VMEM] * 4,
        out_specs=(VMEM, VMEM),
        compiler_params=small,
    )(ids, mine, other, across_part, along_part)


def solution(mesh):
    placed = (
        P("cuts", "slab", "illum"),
        P("cuts", "slab", "illum"),
        P("illum", None, "slab", None),
        P("illum", None),
    )
    return jax.shard_map(
        body,
        mesh=mesh,
        in_specs=placed,
        out_specs=(P("cuts", "slab", "illum"), P("cuts", "slab", "illum")),
        check_vma=False,
    )
```

```python
import functools
import math

import jax
import jax.numpy as jnp
from jax import lax
from jax.experimental import pallas as pl
from jax.experimental.pallas import tpu as pltpu
from jax.sharding import PartitionSpec as P


step_coeff = 0.08
square_coeff = 0.0032
ratio = step_coeff / square_coeff
two_pi = 2.0 * math.pi

HALO = 8
REACH = 16
VMEM = pl.BlockSpec(memory_space=pltpu.VMEM)
SMEM = pl.BlockSpec(memory_space=pltpu.SMEM)
HBM = pl.BlockSpec(memory_space=pltpu.HBM)
small = pltpu.CompilerParams(vmem_limit_bytes=1 << 20)
large = pltpu.CompilerParams(vmem_limit_bytes=8 << 20)


def f32(*shape):
    return jax.ShapeDtypeStruct(shape, jnp.float32)


def lanes_of(shape):
    return lax.broadcasted_iota(jnp.int32, shape, 1)


def turn(x, by):
    by %= 128
    return pltpu.roll(x, by, 1) if by else x


def pack_object(
    ids_ref, phase_ref, atten_ref, measured_ref, angles_ref,
    out_ref, half_ref, head_ref,
    phase, atten, turns, sems,
):
    copies = [
        pltpu.make_async_copy(
            measured_ref.at[0, :, pl.ds(pl.multiple_of(16 * ids_ref[2], 16), 16), :],
            half_ref,
            sems.at[0],
        ),
        pltpu.make_async_copy(angles_ref, turns, sems.at[1]),
        pltpu.make_async_copy(phase_ref, phase, sems.at[2]),
        pltpu.make_async_copy(atten_ref, atten, sems.at[3]),
    ]
    for copy in copies:
        copy.start()
    for copy in copies[1:]:
        copy.wait()
    for n, (ref, layer) in enumerate(((phase, 0), (phase, 1), (atten, 0), (atten, 1))):
        out_ref[:, 32 * n : 32 * n + 32] = ref[layer]
    lane = lanes_of((8, 128))
    head_ref[...] = jnp.where(lane == 0, turns[0, 0], turns[0, 1]).astype(jnp.float32)
    copies[0].wait()


def pack_edges(ids_ref, mine_ref, other_ref, out_ref):
    first = ids_ref[2] == 0
    for pair, (a, b) in enumerate(((mine_ref, other_ref), (other_ref, mine_ref))):
        out_ref[pair] = jnp.where(
            first, jnp.where(first, a[0:8], b[0:8]), jnp.where(first, a[24:32], b[24:32])
        )


def pack_rows(ids_ref, mine_ref, other_ref, edge_ref, out_ref, right_ref, left_ref):
    first = ids_ref[2] == 0
    lane = lanes_of((8, 128))
    spots = 32 * jnp.bitwise_and(lane // 16, 3) + jnp.bitwise_and(lane, 15)
    for block in range(4):
        rows = slice(8 * block, 8 * block + 8)
        both = []
        for pair in range(2):
            refs = (mine_ref, other_ref) if pair == 0 else (other_ref, mine_ref)
            above = refs[0][8 * block - 8 : 8 * block] if block else edge_ref[pair]
            below = refs[1][8 * block + 8 : 8 * block + 16] if block < 3 else edge_ref[pair]
            both.append(jnp.where(first, above, below))
            out_ref[pair, rows] = both[pair]
        for ref, shift in ((right_ref, 16), (left_ref, 0)):
            parts = [picked(x, spots + shift) for x in both]
            ref[rows] = jnp.where(lane < 64, parts[0], parts[1])


def flipped(x):
    rows = 7 - lax.broadcasted_iota(jnp.int32, (8, 128), 0)
    return jnp.take_along_axis(x, rows, axis=0)


def picked(x, lanes):
    return jnp.take_along_axis(x, lanes, axis=1)


def pack_measured(ids_ref, half, head_ref, out_ref, packed, sems):
    lane = lanes_of((8, 128))
    head = head_ref[...]
    zero = jnp.zeros((8, 128), jnp.float32)
    m = jnp.bitwise_and(lane // 16 - ids_ref[0] // 8, 3)
    order = jnp.bitwise_and(lane, 64) + 4 * jnp.bitwise_and(lane, 15) + m
    regs = []
    for comp in range(2):
        first = [half[comp, 0:8, 128 * n : 128 * n + 128] for n in range(8)]
        second = [flipped(half[comp, 8:16, 128 * n : 128 * n + 128]) for n in range(8)]
        regs.append((first, second))
    copies = []
    for j in range(32):
        v, r = divmod(32 * j - REACH, 128)
        for comp in range(2):
            parts = []
            for a in range(2):
                left = regs[comp][a][v] if v >= 0 else zero
                part = turn(left, 64 * a - r)
                if r > 64:
                    right = regs[comp][a][v + 1] if v + 1 < 8 else zero
                    part = jnp.where(lane - 64 * a < 128 - r, part, turn(right, 64 * a - r))
                parts.append(part)
            both = jnp.where(lane < 64, parts[0], parts[1])
            if comp == 0:
                both = jnp.where(lane < 2, head, both)
            packed[j, 8 * comp : 8 * comp + 8] = picked(both, order)
        if j % 8 == 7:
            part = pl.ds(j - 7, 8)
            copies.append(
                pltpu.make_async_copy(packed.at[part], out_ref.at[part], sems.at[j // 8])
            )
            copies[-1].start()
    for copy in copies:
        copy.wait()


def march(
    ids_ref, here_ref, left_ref, right_ref, got_ref,
    mine_ref, other_ref, across_ref, along_ref,
    table, field, stored, sums,
):
    block, slab, cut = ids_ref[0], ids_ref[1], ids_ref[2]
    first = cut == 0
    lane = lanes_of((8, 128))
    sub = lax.broadcasted_iota(jnp.int32, (8, 128), 0)
    upper = lane < 64
    window = jnp.bitwise_and(lane, 63)
    half = jnp.bitwise_and(lane, 64)
    place = jnp.bitwise_and(lane, 15)
    group = jnp.bitwise_and(lane // 16, 3)
    top = 32 * slab + 16 * cut - HALO
    left_column = 32 * block - REACH

    def columns(m):
        return left_column + 4 * place + m

    for q in range(2):
        row = top + jnp.where(upper, 8 * q + sub, 31 - 8 * q - sub)
        row_inside = (row >= 0) & (row < 256)
        column = left_column + window
        inside = row_inside & (column >= 0) & (column < 1024)
        for m in range(4):
            column = columns(m)
            table[8, m, 8 * q : 8 * q + 8] = jnp.where(
                row_inside & (column >= 0) & (column < 1024), square_coeff, 0.0
            )
        for layer in range(4):
            pair, sl = divmod(layer, 2)
            values = []
            for n in (sl, 2 + sl):
                halves = []
                for a, b in ((0, q), (1, 3 - q)):
                    rows = slice(8 * b, 8 * b + 8)
                    at = 64 * (a - pair) - 16 * n
                    halves.append(
                        jnp.where(
                            window < 16,
                            turn(left_ref[rows], at),
                            jnp.where(
                                window < 48,
                                turn(here_ref[pair, rows], 64 * a - 32 * n + 16),
                                turn(right_ref[rows], at + 48),
                            ),
                        )
                    )
                values.append(jnp.where(upper, halves[0], flipped(halves[1])))
            damping = jnp.where(inside, jnp.exp(-values[1]), 0.0)
            re, im = damping * jnp.cos(values[0]), damping * jnp.sin(values[0])
            for m in range(4):
                lanes = half + 4 * place + m
                table[2 * layer, m, 8 * q : 8 * q + 8] = picked(re, lanes)
                table[2 * layer + 1, m, 8 * q : 8 * q + 8] = picked(im, lanes)

    def spread(n, m, r):
        return jnp.broadcast_to(table[n, m, r : r + 1], (8, 128))

    def side(x, m):
        before = x[m - 1] if m else turn(x[3], 1)
        after = x[m + 1] if m < 3 else turn(x[0], 127)
        return before + after

    def diffract(source, begin, inner, orient, emit):
        rows, scaled = {}, {}

        def around(values, r, k, m):
            parts = [values[n][k][m] for n in (r - 1, r + 1) if n in values]
            if r in values:
                parts.append(side(values[r][k], m))
            return functools.reduce(lambda x, y: x + y, parts)

        def scale(r):
            out = []
            for k in range(2):
                new = []
                for m in range(4):
                    total = around(rows, r, k, m)
                    if r in rows:
                        total = total - 4.0 * rows[r][k][m]
                    new.append(spread(8, m, r) * total)
                out.append(new)
            scaled[r] = out

        def finish(r):
            for m in range(4):
                re, im = (-around(scaled, r, k, m) for k in range(2))
                if r in rows:
                    re, im = re + rows[r][0][m], im + rows[r][1][m]
                if r in scaled:
                    mre, mim = scaled[r][0][m], scaled[r][1][m]
                    turned = orient * ratio
                    re = re + (4.0 * mre - turned * mim)
                    im = im + (4.0 * mim + turned * mre)
                emit(r, m, re, im)

        def advance(r):
            if r - 1 >= begin + inner:
                scale(r - 1)
            if r - 2 >= begin + 2 * inner:
                finish(r - 2)

        def opposite(row):
            return [[turn(x, 64) for x in part] for part in row]

        for r in range(begin, 16):
            rows[r] = source(r)
            advance(r)
        rows[16] = opposite(rows[15])
        advance(16)
        scaled[16] = opposite(scaled[15])
        finish(15)

    def received(comp, k):
        parts = [
            got_ref[pl.ds(128 * n + 8 * comp + k, 8, stride=16), :] for n in range(4)
        ]
        out = []
        for m in range(4):
            x = parts[3]
            for n in range(3):
                x = jnp.where(group == (m + n) % 4, parts[n], x)
            if m:
                x = picked(x, half + 16 * jnp.bitwise_and(group + m, 3) + place)
            out.append(x)
        return out

    head = received(0, 0)
    corner = jnp.bitwise_and(lane, 48)
    row_turns = picked(head[0], corner)
    col_turns = picked(head[1], corner)
    row0 = (top + jnp.where(upper, 0, 31)).astype(jnp.float32)
    row_part = row_turns * row0 * (1.0 / 256.0)
    col_part = col_turns * columns(0).astype(jnp.float32) * (1.0 / 1024.0)
    row_part = row_part - jnp.floor(row_part)
    col_part = col_part - jnp.floor(col_part)

    def unit(t):
        return jnp.cos(t), jnp.sin(t)

    def times(a, b):
        return a[0] * b[0] - a[1] * b[1], a[0] * b[1] + a[1] * b[0]

    wave = [unit(two_pi * (row_part + col_part))]
    step = unit(two_pi / 256.0 * row_turns * jnp.where(upper, 1.0, -1.0))
    across = unit(two_pi / 1024.0 * col_turns)
    for _ in range(3):
        wave.append(times(wave[-1], across))
    waves = [wave]

    def from_wave(r):
        while len(waves) <= r:
            waves.append([times(x, step) for x in waves[-1]])
        return [[x[k] for x in waves[r]] for k in range(2)]

    def from_field(r):
        return [[field[k, r, m] for m in range(4)] for k in range(2)]

    def forward(layer):
        def source(r):
            re, im = from_wave(r) if layer == 0 else from_field(r)
            out = ([], [])
            for m in range(4):
                v = times((spread(2 * layer, m, r), spread(2 * layer + 1, m, r)), (re[m], im[m]))
                for k in range(2):
                    stored[2 * layer + k, r, m] = v[k]
                    out[k].append(v[k])
            return out

        measured_rows = {}

        def emit(r, m, re, im):
            if layer < 3:
                field[0, r, m], field[1, r, m] = re, im
                return
            if r not in measured_rows:
                measured_rows[r] = [received(k, r - 8) for k in range(2)]
            column = columns(m)
            keep = (column >= 0) & (column < 1024)
            field[0, r, m] = jnp.where(keep, re - measured_rows[r][0][m], 0.0)
            field[1, r, m] = jnp.where(keep, im - measured_rows[r][1][m], 0.0)

        diffract(source, 2 * layer, 1, 1.0, emit)

    def backward(layer):
        def emit(r, m, re, im):
            vre, vim = stored[2 * layer, r, m], stored[2 * layer + 1, r, m]
            for out, x in enumerate((vre * im - vim * re, -(vre * re) - vim * im)):
                sums[2 * layer + out, m, r : r + 1] = jnp.sum(x, axis=0, keepdims=True)
            if layer:
                a, b = spread(2 * layer, m, r), spread(2 * layer + 1, m, r)
                field[0, r, m], field[1, r, m] = a * re + b * im, a * im - b * re

        diffract(from_field, 2 * layer + 2, -1, -1.0, emit)

    for layer in range(4):
        forward(layer)
        for n in range(2):
            for m in range(4):
                if layer:
                    sums[2 * layer + n, m, 0 : 2 * layer] = jnp.zeros((2 * layer, 128))
    for layer in (3, 2, 1, 0):
        backward(layer)

    spots = half + 48 + window // 4

    def plain(n, q):
        out = None
        for m in range(4):
            x = sums[n, m, 8 * q : 8 * q + 8]
            x = x + turn(x, 16)
            x = picked(x + turn(x, 32), spots)
            out = x if out is None else jnp.where(jnp.bitwise_and(lane, 3) == m, x, out)
        return out

    blocks = [[None] * 4 for _ in range(2)]
    for pair in range(2):
        for q in range(2):
            for n in range(4):
                out, sl = divmod(n, 2)
                x = plain(2 * (2 * pair + sl) + out, q)
                for b, y in ((q, turn(x, 32 * n - 16)), (3 - q, turn(x, 32 * n - 80))):
                    old = blocks[pair][b]
                    blocks[pair][b] = y if old is None else jnp.where(lane < 32 * n, old, y)
        for b in (2, 3):
            blocks[pair][b] = flipped(blocks[pair][b])
    mine = [jnp.where(first, a, b) for a, b in zip(*blocks)]
    other = [jnp.where(first, b, a) for a, b in zip(*blocks)]
    none = jnp.zeros((8, 128), jnp.float32)
    for parts, ref in ((mine, mine_ref), (other, other_ref)):
        for b in range(4):
            ref[8 * b : 8 * b + 8] = jnp.where(
                first, parts[b + 1] if b < 3 else none, parts[b - 1] if b > 0 else none
            )
    across_ref[...] = jnp.where(first, other[0], other[3])
    along_ref[...] = jnp.where(first, mine[0], mine[3])


def combine(ids_ref, mine_ref, other_ref, across_ref, along_ref, phase_ref, atten_ref):
    first = ids_ref[2] == 0
    for b in range(4):
        rows = slice(8 * b, 8 * b + 8)
        total = mine_ref[rows] + other_ref[rows]
        if b == 0:
            total = total + jnp.where(first, across_ref[...], along_ref[...])
        if b == 3:
            total = total + jnp.where(first, along_ref[...], across_ref[...])
        for sl in range(2):
            phase_ref[sl, rows] = turn(total, -32 * sl)[:, 0:32]
            atten_ref[sl, rows] = turn(total, -64 - 32 * sl)[:, 0:32]


def body(phase_delay, attenuation, measured, angles):
    block = lax.axis_index("illum")
    slab = lax.axis_index("slab")
    cut = lax.axis_index("cuts")
    ids = jnp.stack([block, slab, cut]).astype(jnp.int32)
    n_slabs, n_blocks = lax.axis_size("slab"), lax.axis_size("illum")
    rows_axis = ("slab", "cuts")

    def both_ways(pairs):
        return pairs + [(b, a) for a, b in pairs]

    partner = both_ways([(2 * s, 2 * s + 1) for s in range(n_slabs)])
    across = both_ways([(2 * s + 1, 2 * s + 2) for s in range(n_slabs - 1)])
    along = [(2 * s + 1, 2 * s + 3) for s in range(n_slabs - 1)]
    along += [(2 * s + 2, 2 * s) for s in range(n_slabs - 1)]

    phase_delay, attenuation, measured, angles = (
        pltpu.with_memory_space_constraint(x, pltpu.HBM)
        for x in (phase_delay, attenuation, measured, angles)
    )
    mine, half, head = pl.pallas_call(
        pack_object,
        out_shape=(f32(32, 128), f32(2, 16, 1024), f32(8, 128)),
        in_specs=[SMEM] + [HBM] * 4,
        out_specs=(VMEM,) * 3,
        scratch_shapes=[
            pltpu.VMEM((2, 32, 32), jnp.float32),
            pltpu.VMEM((2, 32, 32), jnp.float32),
            pltpu.SMEM((1, 2), jnp.int32),
            pltpu.SemaphoreType.DMA((4,)),
        ],
        compiler_params=small,
    )(ids, phase_delay, attenuation, measured, angles)
    other = lax.ppermute(mine, rows_axis, partner)
    sent = pl.pallas_call(
        pack_measured,
        out_shape=f32(32, 16, 128),
        in_specs=[SMEM, VMEM, VMEM],
        out_specs=HBM,
        scratch_shapes=[
            pltpu.VMEM((32, 16, 128), jnp.float32),
            pltpu.SemaphoreType.DMA((4,)),
        ],
        compiler_params=small,
    )(ids, half, head)
    edges = pl.pallas_call(
        pack_edges,
        out_shape=f32(2, 8, 128),
        in_specs=[SMEM, VMEM, VMEM],
        out_specs=VMEM,
        compiler_params=small,
    )(ids, mine, other)
    edges = lax.ppermute(edges, rows_axis, across)
    got = lax.all_to_all(sent, "illum", 0, 0, tiled=True)
    here, to_right, to_left = pl.pallas_call(
        pack_rows,
        out_shape=(f32(2, 32, 128), f32(32, 128), f32(32, 128)),
        in_specs=[SMEM] + [VMEM] * 3,
        out_specs=(VMEM,) * 3,
        compiler_params=small,
    )(ids, mine, other, edges)
    from_left = lax.ppermute(to_right, "illum", [(i, i + 1) for i in range(n_blocks - 1)])
    from_right = lax.ppermute(to_left, "illum", [(i + 1, i) for i in range(n_blocks - 1)])

    mine, other, across_part, along_part = pl.pallas_call(
        march,
        out_shape=(f32(32, 128), f32(32, 128), f32(8, 128), f32(8, 128)),
        in_specs=[SMEM] + [VMEM] * 4,
        out_specs=(VMEM,) * 4,
        scratch_shapes=[
            pltpu.VMEM((9, 4, 16, 128), jnp.float32),
            pltpu.VMEM((2, 16, 4, 8, 128), jnp.float32),
            pltpu.VMEM((8, 16, 4, 8, 128), jnp.float32),
            pltpu.VMEM((8, 4, 16, 128), jnp.float32),
        ],
        compiler_params=large,
    )(ids, here, from_left, from_right, got.reshape(512, 128))
    other = lax.ppermute(other, rows_axis, partner)
    across_part = lax.ppermute(across_part, rows_axis, across)
    along_part = lax.ppermute(along_part, rows_axis, along)
    return pl.pallas_call(
        combine,
        out_shape=(f32(2, 32, 32), f32(2, 32, 32)),
        in_specs=[SMEM] + [VMEM] * 4,
        out_specs=(VMEM, VMEM),
        compiler_params=small,
    )(ids, mine, other, across_part, along_part)


def solution(mesh):
    placed = (
        P("cuts", "slab", "illum"),
        P("cuts", "slab", "illum"),
        P("illum", None, "slab", None),
        P("illum", None),
    )
    return jax.shard_map(
        body,
        mesh=mesh,
        in_specs=placed,
        out_specs=(P("cuts", "slab", "illum"), P("cuts", "slab", "illum")),
        check_vma=False,
    )
```

```python
import functools
import math

import jax
import jax.numpy as jnp
from jax import lax
from jax.experimental import pallas as pl
from jax.experimental.pallas import tpu as pltpu
from jax.sharding import PartitionSpec as P


step_coeff = 0.08
square_coeff = 0.0032
ratio = step_coeff / square_coeff
two_pi = 2.0 * math.pi

HALO = 8
REACH = 16
VMEM = pl.BlockSpec(memory_space=pltpu.VMEM)
SMEM = pl.BlockSpec(memory_space=pltpu.SMEM)
HBM = pl.BlockSpec(memory_space=pltpu.HBM)
small = pltpu.CompilerParams(vmem_limit_bytes=1 << 20)
large = pltpu.CompilerParams(vmem_limit_bytes=8 << 20)


def f32(*shape):
    return jax.ShapeDtypeStruct(shape, jnp.float32)


def lanes_of(shape):
    return lax.broadcasted_iota(jnp.int32, shape, 1)


def turn(x, by):
    by %= 128
    return pltpu.roll(x, by, 1) if by else x


def pack_object(
    ids_ref, phase_ref, atten_ref, measured_ref, angles_ref,
    out_ref, half_ref, head_ref, place_ref,
    phase, atten, turns, sems,
):
    copies = [
        pltpu.make_async_copy(
            measured_ref.at[0, :, pl.ds(pl.multiple_of(16 * ids_ref[2], 16), 16), :],
            half_ref,
            sems.at[0],
        ),
        pltpu.make_async_copy(angles_ref, turns, sems.at[1]),
        pltpu.make_async_copy(phase_ref, phase, sems.at[2]),
        pltpu.make_async_copy(atten_ref, atten, sems.at[3]),
    ]
    for copy in copies:
        copy.start()
    for n in range(3):
        place_ref[n] = jnp.full((8, 128), ids_ref[n], jnp.int32)
    for copy in copies[1:]:
        copy.wait()
    for n, (ref, layer) in enumerate(((phase, 0), (phase, 1), (atten, 0), (atten, 1))):
        out_ref[:, 32 * n : 32 * n + 32] = ref[layer]
    lane = lanes_of((8, 128))
    head_ref[...] = jnp.where(lane == 0, turns[0, 0], turns[0, 1]).astype(jnp.float32)
    copies[0].wait()


def pack_edges(place_ref, mine_ref, other_ref, out_ref):
    first = place_ref[2] == 0
    for pair, (a, b) in enumerate(((mine_ref, other_ref), (other_ref, mine_ref))):
        out_ref[pair] = jnp.where(
            first, jnp.where(first, a[0:8], b[0:8]), jnp.where(first, a[24:32], b[24:32])
        )


def pack_rows(place_ref, mine_ref, other_ref, edge_ref, out_ref, right_ref, left_ref):
    first = place_ref[2] == 0
    lane = lanes_of((8, 128))
    spots = 32 * jnp.bitwise_and(lane // 16, 3) + jnp.bitwise_and(lane, 15)
    for block in range(4):
        rows = slice(8 * block, 8 * block + 8)
        both = []
        for pair in range(2):
            refs = (mine_ref, other_ref) if pair == 0 else (other_ref, mine_ref)
            above = refs[0][8 * block - 8 : 8 * block] if block else edge_ref[pair]
            below = refs[1][8 * block + 8 : 8 * block + 16] if block < 3 else edge_ref[pair]
            both.append(jnp.where(first, above, below))
            out_ref[pair, rows] = both[pair]
        for ref, shift in ((right_ref, 16), (left_ref, 0)):
            parts = [picked(x, spots + shift) for x in both]
            ref[rows] = jnp.where(lane < 64, parts[0], parts[1])


def flipped(x):
    rows = 7 - lax.broadcasted_iota(jnp.int32, (8, 128), 0)
    return jnp.take_along_axis(x, rows, axis=0)


def picked(x, lanes):
    return jnp.take_along_axis(x, lanes, axis=1)


def thirds(x):
    parts = []
    for _ in range(3):
        part = x.astype(jnp.bfloat16)
        x = x - part.astype(jnp.float32)
        parts.append(part)
    return jnp.concatenate(parts, axis=1)


def permuted(x, chosen):
    ones = jnp.where(chosen, 1.0, 0.0).astype(jnp.bfloat16)
    return jnp.dot(
        thirds(x),
        jnp.concatenate([ones] * 3, axis=0),
        preferred_element_type=jnp.float32,
    )


def square_iotas(width=128):
    shape = (128, width)
    return lax.broadcasted_iota(jnp.int32, shape, 0), lanes_of(shape)


def pack_measured(place_ref, half, head_ref, out_ref, plain, packed, sems):
    lane = lanes_of((8, 128))
    head = head_ref[...]
    zero = jnp.zeros((8, 128), jnp.float32)
    source, target = square_iotas()
    m = jnp.bitwise_and(target // 16 - jnp.tile(place_ref[0] // 8, (16, 1)), 3)
    chosen = source == jnp.bitwise_and(target, 64) + 4 * jnp.bitwise_and(target, 15) + m
    regs = []
    for comp in range(2):
        first = [half[comp, 0:8, 128 * n : 128 * n + 128] for n in range(8)]
        second = [flipped(half[comp, 8:16, 128 * n : 128 * n + 128]) for n in range(8)]
        regs.append((first, second))
    copies = []
    for j in range(32):
        v, r = divmod(32 * j - REACH, 128)
        for comp in range(2):
            parts = []
            for a in range(2):
                left = regs[comp][a][v] if v >= 0 else zero
                part = turn(left, 64 * a - r)
                if r > 64:
                    right = regs[comp][a][v + 1] if v + 1 < 8 else zero
                    part = jnp.where(lane - 64 * a < 128 - r, part, turn(right, 64 * a - r))
                parts.append(part)
            both = jnp.where(lane < 64, parts[0], parts[1])
            if comp == 0:
                both = jnp.where(lane < 2, head, both)
            plain[16 * j + 8 * comp : 16 * j + 8 * comp + 8] = both
        if j % 8 == 7:
            part = pl.ds(j - 7, 8)
            moved = permuted(plain[16 * j - 112 : 16 * j + 16], chosen)
            packed[part] = moved.reshape(8, 16, 128)
            copies.append(
                pltpu.make_async_copy(packed.at[part], out_ref.at[part], sems.at[j // 8])
            )
            copies[-1].start()
    for copy in copies:
        copy.wait()


def march(
    place_ref, here_ref, left_ref, right_ref, got_ref,
    mine_ref, other_ref, across_ref, along_ref,
    table, flat, field, stored, sums,
):
    block, slab, cut = place_ref[0], place_ref[1], place_ref[2]
    first = cut == 0
    lane = lanes_of((8, 128))
    sub = lax.broadcasted_iota(jnp.int32, (8, 128), 0)
    upper = lane < 64
    window = jnp.bitwise_and(lane, 63)
    half = jnp.bitwise_and(lane, 64)
    place = jnp.bitwise_and(lane, 15)
    group = jnp.bitwise_and(lane // 16, 3)
    top = 32 * slab + 16 * cut - HALO
    left_column = 32 * block - REACH

    def columns(m):
        return left_column + 4 * place + m

    for q in range(2):
        row = top + jnp.where(upper, 8 * q + sub, 31 - 8 * q - sub)
        row_inside = (row >= 0) & (row < 256)
        column = left_column + window
        inside = row_inside & (column >= 0) & (column < 1024)
        for m in range(4):
            column = columns(m)
            table[8, m, 8 * q : 8 * q + 8] = jnp.where(
                row_inside & (column >= 0) & (column < 1024), square_coeff, 0.0
            )
        for layer in range(4):
            pair, sl = divmod(layer, 2)
            values = []
            for n in (sl, 2 + sl):
                halves = []
                for a, b in ((0, q), (1, 3 - q)):
                    rows = slice(8 * b, 8 * b + 8)
                    at = 64 * (a - pair) - 16 * n
                    halves.append(
                        jnp.where(
                            window < 16,
                            turn(left_ref[rows], at),
                            jnp.where(
                                window < 48,
                                turn(here_ref[pair, rows], 64 * a - 32 * n + 16),
                                turn(right_ref[rows], at + 48),
                            ),
                        )
                    )
                values.append(jnp.where(upper, halves[0], flipped(halves[1])))
            damping = jnp.where(inside, jnp.exp(-values[1]), 0.0)
            re, im = damping * jnp.cos(values[0]), damping * jnp.sin(values[0])
            flat[32 * layer + 8 * q : 32 * layer + 8 * q + 8] = re
            flat[32 * layer + 8 * q + 16 : 32 * layer + 8 * q + 24] = im
    source, target = square_iotas(512)
    spot = jnp.bitwise_and(target, 64) + 4 * jnp.bitwise_and(target, 15) + target // 128
    wide = permuted(flat[...], source == spot)
    for m in range(4):
        table[0:8, m] = wide[:, 128 * m : 128 * m + 128].reshape(8, 16, 128)

    def spread(n, m, r):
        return jnp.broadcast_to(table[n, m, r : r + 1], (8, 128))

    def side(x, m):
        before = x[m - 1] if m else turn(x[3], 1)
        after = x[m + 1] if m < 3 else turn(x[0], 127)
        return before + after

    def diffract(source, begin, inner, orient, emit):
        rows, scaled = {}, {}

        def around(values, r, k, m):
            parts = [values[n][k][m] for n in (r - 1, r + 1) if n in values]
            if r in values:
                parts.append(side(values[r][k], m))
            return functools.reduce(lambda x, y: x + y, parts)

        def scale(r):
            out = []
            for k in range(2):
                new = []
                for m in range(4):
                    total = around(rows, r, k, m)
                    if r in rows:
                        total = total - 4.0 * rows[r][k][m]
                    new.append(spread(8, m, r) * total)
                out.append(new)
            scaled[r] = out

        def finish(r):
            for m in range(4):
                re, im = (around(scaled, r, k, m) for k in range(2))
                if r in rows:
                    re, im = rows[r][0][m] - re, rows[r][1][m] - im
                else:
                    re, im = -re, -im
                if r in scaled:
                    mre, mim = scaled[r][0][m], scaled[r][1][m]
                    turned = orient * ratio
                    re = re + (4.0 * mre - turned * mim)
                    im = im + (4.0 * mim + turned * mre)
                emit(r, m, re, im)

        def advance(r):
            if r - 1 >= begin + inner:
                scale(r - 1)
            if r - 2 >= begin + 2 * inner:
                finish(r - 2)

        def opposite(row):
            return [[turn(x, 64) for x in part] for part in row]

        for r in range(begin, 16):
            rows[r] = source(r)
            advance(r)
        rows[16] = opposite(rows[15])
        advance(16)
        scaled[16] = opposite(scaled[15])
        finish(15)

    def received(comp, k):
        parts = [
            got_ref[pl.ds(128 * n + 8 * comp + k, 8, stride=16), :] for n in range(4)
        ]
        out = []
        for m in range(4):
            x = parts[3]
            for n in range(3):
                x = jnp.where(group == (m + n) % 4, parts[n], x)
            if m:
                x = picked(x, half + 16 * jnp.bitwise_and(group + m, 3) + place)
            out.append(x)
        return out

    head = received(0, 0)
    corner = jnp.bitwise_and(lane, 48)
    row_turns = picked(head[0], corner)
    col_turns = picked(head[1], corner)
    row0 = (top + jnp.where(upper, 0, 31)).astype(jnp.float32)
    row_part = row_turns * row0 * (1.0 / 256.0)
    col_part = col_turns * columns(0).astype(jnp.float32) * (1.0 / 1024.0)
    row_part = row_part - jnp.floor(row_part)
    col_part = col_part - jnp.floor(col_part)

    def unit(t):
        return jnp.cos(t), jnp.sin(t)

    def times(a, b):
        return a[0] * b[0] - a[1] * b[1], a[0] * b[1] + a[1] * b[0]

    wave = [unit(two_pi * (row_part + col_part))]
    step = unit(two_pi / 256.0 * row_turns * jnp.where(upper, 1.0, -1.0))
    across = unit(two_pi / 1024.0 * col_turns)
    for _ in range(3):
        wave.append(times(wave[-1], across))
    waves = [wave]

    def from_wave(r):
        while len(waves) <= r:
            waves.append([times(x, step) for x in waves[-1]])
        return [[x[k] for x in waves[r]] for k in range(2)]

    def from_field(r):
        return [[field[k, r, m] for m in range(4)] for k in range(2)]

    def forward(layer):
        def source(r):
            re, im = from_wave(r) if layer == 0 else from_field(r)
            out = ([], [])
            for m in range(4):
                v = times((spread(2 * layer, m, r), spread(2 * layer + 1, m, r)), (re[m], im[m]))
                for k in range(2):
                    stored[2 * layer + k, r, m] = v[k]
                    out[k].append(v[k])
            return out

        measured_rows = {}

        def emit(r, m, re, im):
            if layer < 3:
                field[0, r, m], field[1, r, m] = re, im
                return
            if r not in measured_rows:
                measured_rows[r] = [received(k, r - 8) for k in range(2)]
            column = columns(m)
            keep = (column >= 0) & (column < 1024)
            field[0, r, m] = jnp.where(keep, re - measured_rows[r][0][m], 0.0)
            field[1, r, m] = jnp.where(keep, im - measured_rows[r][1][m], 0.0)

        diffract(source, 2 * layer, 1, 1.0, emit)

    def backward(layer):
        def emit(r, m, re, im):
            vre, vim = stored[2 * layer, r, m], stored[2 * layer + 1, r, m]
            for out, x in enumerate((vre * im - vim * re, vre * re + vim * im)):
                sums[2 * layer + out, m, r : r + 1] = jnp.sum(x, axis=0, keepdims=True)
            if layer:
                a, b = spread(2 * layer, m, r), spread(2 * layer + 1, m, r)
                field[0, r, m], field[1, r, m] = a * re + b * im, a * im - b * re

        diffract(from_field, 2 * layer + 2, -1, -1.0, emit)

    for layer in range(4):
        forward(layer)
        for n in range(2):
            for m in range(4):
                if layer:
                    sums[2 * layer + n, m, 0 : 2 * layer] = jnp.zeros((2 * layer, 128))
    for layer in (3, 2, 1, 0):
        backward(layer)

    source, target = square_iotas()
    near = (jnp.bitwise_and(source, 64) == jnp.bitwise_and(target, 64)) & (
        jnp.bitwise_and(source, 15) == jnp.bitwise_and(target, 63) // 4
    )
    total = None
    for m in range(4):
        x = sums[:, m].reshape(128, 128)
        x = permuted(x, near & (jnp.bitwise_and(target, 3) == m))
        total = x if total is None else total + x
    flat[...] = total

    def plain(n, q):
        return flat[16 * n + 8 * q : 16 * n + 8 * q + 8]

    blocks = [[None] * 4 for _ in range(2)]
    for pair in range(2):
        for q in range(2):
            for n in range(4):
                out, sl = divmod(n, 2)
                x = plain(2 * (2 * pair + sl) + out, q)
                x = -x if out else x
                for b, y in ((q, turn(x, 32 * n - 16)), (3 - q, turn(x, 32 * n - 80))):
                    old = blocks[pair][b]
                    blocks[pair][b] = y if old is None else jnp.where(lane < 32 * n, old, y)
        for b in (2, 3):
            blocks[pair][b] = flipped(blocks[pair][b])
    mine = [jnp.where(first, a, b) for a, b in zip(*blocks)]
    other = [jnp.where(first, b, a) for a, b in zip(*blocks)]
    none = jnp.zeros((8, 128), jnp.float32)
    for parts, ref in ((mine, mine_ref), (other, other_ref)):
        for b in range(4):
            ref[8 * b : 8 * b + 8] = jnp.where(
                first, parts[b + 1] if b < 3 else none, parts[b - 1] if b > 0 else none
            )
    across_ref[...] = jnp.where(first, other[0], other[3])
    along_ref[...] = jnp.where(first, mine[0], mine[3])


def combine(place_ref, mine_ref, other_ref, across_ref, along_ref, phase_ref, atten_ref):
    first = place_ref[2] == 0
    for b in range(4):
        rows = slice(8 * b, 8 * b + 8)
        total = mine_ref[rows] + other_ref[rows]
        if b == 0:
            total = total + jnp.where(first, across_ref[...], along_ref[...])
        if b == 3:
            total = total + jnp.where(first, along_ref[...], across_ref[...])
        for sl in range(2):
            phase_ref[sl, rows] = turn(total, -32 * sl)[:, 0:32]
            atten_ref[sl, rows] = turn(total, -64 - 32 * sl)[:, 0:32]


def body(phase_delay, attenuation, measured, angles):
    block = lax.axis_index("illum")
    slab = lax.axis_index("slab")
    cut = lax.axis_index("cuts")
    ids = jnp.stack([block, slab, cut]).astype(jnp.int32)
    n_slabs, n_blocks = lax.axis_size("slab"), lax.axis_size("illum")
    rows_axis = ("slab", "cuts")

    def both_ways(pairs):
        return pairs + [(b, a) for a, b in pairs]

    partner = both_ways([(2 * s, 2 * s + 1) for s in range(n_slabs)])
    across = both_ways([(2 * s + 1, 2 * s + 2) for s in range(n_slabs - 1)])
    along = [(2 * s + 1, 2 * s + 3) for s in range(n_slabs - 1)]
    along += [(2 * s + 2, 2 * s) for s in range(n_slabs - 1)]

    phase_delay, attenuation, measured, angles = (
        pltpu.with_memory_space_constraint(x, pltpu.HBM)
        for x in (phase_delay, attenuation, measured, angles)
    )
    mine, half, head, place = pl.pallas_call(
        pack_object,
        out_shape=(
            f32(32, 128),
            f32(2, 16, 1024),
            f32(8, 128),
            jax.ShapeDtypeStruct((3, 8, 128), jnp.int32),
        ),
        in_specs=[SMEM] + [HBM] * 4,
        out_specs=(VMEM,) * 4,
        scratch_shapes=[
            pltpu.VMEM((2, 32, 32), jnp.float32),
            pltpu.VMEM((2, 32, 32), jnp.float32),
            pltpu.SMEM((1, 2), jnp.int32),
            pltpu.SemaphoreType.DMA((4,)),
        ],
        compiler_params=small,
    )(ids, phase_delay, attenuation, measured, angles)
    other = lax.ppermute(mine, rows_axis, partner)
    sent = pl.pallas_call(
        pack_measured,
        out_shape=f32(32, 16, 128),
        in_specs=[VMEM] * 3,
        out_specs=HBM,
        scratch_shapes=[
            pltpu.VMEM((512, 128), jnp.float32),
            pltpu.VMEM((32, 16, 128), jnp.float32),
            pltpu.SemaphoreType.DMA((4,)),
        ],
        compiler_params=small,
    )(place, half, head)
    edges = pl.pallas_call(
        pack_edges,
        out_shape=f32(2, 8, 128),
        in_specs=[VMEM] * 3,
        out_specs=VMEM,
        compiler_params=small,
    )(place, mine, other)
    edges = lax.ppermute(edges, rows_axis, across)
    got = lax.all_to_all(sent, "illum", 0, 0, tiled=True)
    here, to_right, to_left = pl.pallas_call(
        pack_rows,
        out_shape=(f32(2, 32, 128), f32(32, 128), f32(32, 128)),
        in_specs=[VMEM] * 4,
        out_specs=(VMEM,) * 3,
        compiler_params=small,
    )(place, mine, other, edges)
    from_left = lax.ppermute(to_right, "illum", [(i, i + 1) for i in range(n_blocks - 1)])
    from_right = lax.ppermute(to_left, "illum", [(i + 1, i) for i in range(n_blocks - 1)])

    mine, other, across_part, along_part = pl.pallas_call(
        march,
        out_shape=(f32(32, 128), f32(32, 128), f32(8, 128), f32(8, 128)),
        in_specs=[VMEM] * 5,
        out_specs=(VMEM,) * 4,
        scratch_shapes=[
            pltpu.VMEM((9, 4, 16, 128), jnp.float32),
            pltpu.VMEM((128, 128), jnp.float32),
            pltpu.VMEM((2, 16, 4, 8, 128), jnp.float32),
            pltpu.VMEM((8, 16, 4, 8, 128), jnp.float32),
            pltpu.VMEM((8, 4, 16, 128), jnp.float32),
        ],
        compiler_params=large,
    )(place, here, from_left, from_right, got.reshape(512, 128))
    other = lax.ppermute(other, rows_axis, partner)
    across_part = lax.ppermute(across_part, rows_axis, across)
    along_part = lax.ppermute(along_part, rows_axis, along)
    return pl.pallas_call(
        combine,
        out_shape=(f32(2, 32, 32), f32(2, 32, 32)),
        in_specs=[VMEM] * 5,
        out_specs=(VMEM, VMEM),
        compiler_params=small,
    )(place, mine, other, across_part, along_part)


def solution(mesh):
    placed = (
        P("cuts", "slab", "illum"),
        P("cuts", "slab", "illum"),
        P("illum", None, "slab", None),
        P("illum", None),
    )
    return jax.shard_map(
        body,
        mesh=mesh,
        in_specs=placed,
        out_specs=(P("cuts", "slab", "illum"), P("cuts", "slab", "illum")),
        check_vma=False,
    )
```

```python
import functools
import math

import jax
import jax.numpy as jnp
from jax import lax
from jax.experimental import pallas as pl
from jax.experimental.pallas import tpu as pltpu
from jax.sharding import PartitionSpec as P


step_coeff = 0.08
square_coeff = 0.0032
ratio = step_coeff / square_coeff
two_pi = 2.0 * math.pi

HALO = 8
REACH = 16
VMEM = pl.BlockSpec(memory_space=pltpu.VMEM)
SMEM = pl.BlockSpec(memory_space=pltpu.SMEM)
HBM = pl.BlockSpec(memory_space=pltpu.HBM)
small = pltpu.CompilerParams(vmem_limit_bytes=1 << 20)
large = pltpu.CompilerParams(vmem_limit_bytes=8 << 20)


def f32(*shape):
    return jax.ShapeDtypeStruct(shape, jnp.float32)


def lanes_of(shape):
    return lax.broadcasted_iota(jnp.int32, shape, 1)


def turn(x, by):
    by %= 128
    return pltpu.roll(x, by, 1) if by else x


def pack_object(
    phase_ref, atten_ref, measured_ref, angles_ref,
    out_ref, whole_ref, head_ref,
    phase, atten, turns, sems,
):
    copies = [
        pltpu.make_async_copy(phase_ref, phase, sems.at[0]),
        pltpu.make_async_copy(atten_ref, atten, sems.at[1]),
        pltpu.make_async_copy(angles_ref, turns, sems.at[2]),
        pltpu.make_async_copy(measured_ref.at[0], whole_ref, sems.at[3]),
    ]
    for copy in copies:
        copy.start()
    for copy in copies[:3]:
        copy.wait()
    for n, (ref, layer) in enumerate(((phase, 0), (phase, 1), (atten, 0), (atten, 1))):
        out_ref[:, 32 * n : 32 * n + 32] = ref[layer]
    lane = lanes_of((8, 128))
    head_ref[...] = jnp.where(lane == 0, turns[0, 0], turns[0, 1]).astype(jnp.float32)
    copies[3].wait()


def pairs_of(first, mine_ref, other_ref, rows):
    mine, other = mine_ref[rows], other_ref[rows]
    return [jnp.where(first, mine, other), jnp.where(first, other, mine)]


def sides_of(first, near_ref, far_ref, rows):
    near, far = near_ref[rows], far_ref[rows]
    return [jnp.where(first, near, far), jnp.where(first, far, near)]


def pack_sides(place_ref, mine_ref, other_ref, out_ref):
    first = place_ref[2] == 0
    lane = lanes_of((8, 128))
    spots = 32 * jnp.bitwise_and(lane // 16, 3) + jnp.bitwise_and(lane, 15)
    for block in range(4):
        rows = slice(8 * block, 8 * block + 8)
        both = pairs_of(first, mine_ref, other_ref, rows)
        left, right = (
            jnp.where(lane < 64, *(picked(x, spots + shift) for x in both)) for shift in (0, 16)
        )
        out_ref[rows] = jnp.where(first, left, right)


def pack_edges(place_ref, mine_ref, other_ref, near_ref, far_ref, out_ref):
    first = place_ref[2] == 0
    for n, (of, refs) in enumerate(
        ((pairs_of, (mine_ref, other_ref)), (sides_of, (near_ref, far_ref)))
    ):
        top, bottom = (of(first, *refs, rows) for rows in (slice(0, 8), slice(24, 32)))
        for k in range(2):
            out_ref[2 * n + k] = jnp.where(first, top[k], bottom[k])


def pack_rows(
    place_ref, mine_ref, other_ref, near_ref, far_ref, edge_ref, out_ref, left_ref, right_ref
):
    first = place_ref[2] == 0
    blocks = []
    for block in range(4):
        rows = slice(8 * block, 8 * block + 8)
        blocks.append(
            pairs_of(first, mine_ref, other_ref, rows)
            + sides_of(first, near_ref, far_ref, rows)
        )
    for block in range(4):
        rows = slice(8 * block, 8 * block + 8)
        new = []
        for k in range(4):
            above = blocks[block - 1][k] if block else edge_ref[k]
            below = blocks[block + 1][k] if block < 3 else edge_ref[k]
            new.append(jnp.where(first, above, below))
        out_ref[0, rows], out_ref[1, rows], left_ref[rows], right_ref[rows] = new


def flipped(x):
    rows = 7 - lax.broadcasted_iota(jnp.int32, (8, 128), 0)
    return jnp.take_along_axis(x, rows, axis=0)


def picked(x, lanes):
    return jnp.take_along_axis(x, lanes, axis=1)


def thirds(x):
    parts = []
    for _ in range(3):
        part = x.astype(jnp.bfloat16)
        x = x - part.astype(jnp.float32)
        parts.append(part)
    return jnp.concatenate(parts, axis=1)


def permuted(x, chosen):
    ones = jnp.where(chosen, 1.0, 0.0).astype(jnp.bfloat16)
    return jnp.dot(
        thirds(x),
        jnp.concatenate([ones] * 3, axis=0),
        preferred_element_type=jnp.float32,
    )


def square_iotas(width=128):
    shape = (128, width)
    return lax.broadcasted_iota(jnp.int32, shape, 0), lanes_of(shape)


def pack_measured(place_ref, whole_ref, head_ref, out_ref, plain, packed, sems):
    lane = lanes_of((8, 128))
    head = head_ref[...]
    zero = jnp.zeros((8, 128), jnp.float32)
    source, target = square_iotas()
    m = jnp.bitwise_and(target // 16 - jnp.tile(place_ref[0] // 8, (16, 1)), 3)
    chosen = source == jnp.bitwise_and(target, 64) + 4 * jnp.bitwise_and(target, 15) + m
    cut = place_ref[2]
    regs = []
    for comp in range(2):
        rows = []
        for a in range(2):
            rows.append([])
            for n in range(8):
                at = slice(128 * n, 128 * n + 128)
                x = jnp.where(
                    cut == 0,
                    whole_ref[comp, 8 * a : 8 * a + 8, at],
                    whole_ref[comp, 8 * a + 16 : 8 * a + 24, at],
                )
                rows[a].append(flipped(x) if a else x)
        regs.append(rows)
    copies = []
    for j in range(32):
        v, r = divmod(32 * j - REACH, 128)
        for comp in range(2):
            parts = []
            for a in range(2):
                left = regs[comp][a][v] if v >= 0 else zero
                part = turn(left, 64 * a - r)
                if r > 64:
                    right = regs[comp][a][v + 1] if v + 1 < 8 else zero
                    part = jnp.where(lane - 64 * a < 128 - r, part, turn(right, 64 * a - r))
                parts.append(part)
            both = jnp.where(lane < 64, parts[0], parts[1])
            if comp == 0:
                both = jnp.where(lane < 2, head, both)
            plain[16 * j + 8 * comp : 16 * j + 8 * comp + 8] = both
        if j % 8 == 7:
            part = pl.ds(j - 7, 8)
            moved = permuted(plain[16 * j - 112 : 16 * j + 16], chosen)
            packed[part] = moved.reshape(8, 16, 128)
            copies.append(
                pltpu.make_async_copy(packed.at[part], out_ref.at[part], sems.at[j // 8])
            )
            copies[-1].start()
    for copy in copies:
        copy.wait()


def march(
    place_ref, here_ref, left_ref, right_ref, got_ref,
    mine_ref, other_ref, edge_ref,
    table, flat, field, stored, sums,
):
    block, slab, cut = place_ref[0], place_ref[1], place_ref[2]
    first = cut == 0
    lane = lanes_of((8, 128))
    sub = lax.broadcasted_iota(jnp.int32, (8, 128), 0)
    upper = lane < 64
    window = jnp.bitwise_and(lane, 63)
    half = jnp.bitwise_and(lane, 64)
    place = jnp.bitwise_and(lane, 15)
    group = jnp.bitwise_and(lane // 16, 3)
    top = 32 * slab + 16 * cut - HALO
    left_column = 32 * block - REACH

    def columns(m):
        return left_column + 4 * place + m

    for q in range(2):
        row = top + jnp.where(upper, 8 * q + sub, 31 - 8 * q - sub)
        row_inside = (row >= 0) & (row < 256)
        column = left_column + window
        inside = row_inside & (column >= 0) & (column < 1024)
        for m in range(4):
            column = columns(m)
            table[8, m, 8 * q : 8 * q + 8] = jnp.where(
                row_inside & (column >= 0) & (column < 1024), square_coeff, 0.0
            )
        for layer in range(4):
            pair, sl = divmod(layer, 2)
            values = []
            for n in (sl, 2 + sl):
                halves = []
                for a, b in ((0, q), (1, 3 - q)):
                    rows = slice(8 * b, 8 * b + 8)
                    at = 64 * (a - pair) - 16 * n
                    halves.append(
                        jnp.where(
                            window < 16,
                            turn(left_ref[rows], at),
                            jnp.where(
                                window < 48,
                                turn(here_ref[pair, rows], 64 * a - 32 * n + 16),
                                turn(right_ref[rows], at + 48),
                            ),
                        )
                    )
                values.append(jnp.where(upper, halves[0], flipped(halves[1])))
            damping = jnp.where(inside, jnp.exp(-values[1]), 0.0)
            re, im = damping * jnp.cos(values[0]), damping * jnp.sin(values[0])
            flat[32 * layer + 8 * q : 32 * layer + 8 * q + 8] = re
            flat[32 * layer + 8 * q + 16 : 32 * layer + 8 * q + 24] = im
    source, target = square_iotas(512)
    spot = jnp.bitwise_and(target, 64) + 4 * jnp.bitwise_and(target, 15) + target // 128
    wide = permuted(flat[...], source == spot)
    for m in range(4):
        table[0:8, m] = wide[:, 128 * m : 128 * m + 128].reshape(8, 16, 128)

    def spread(n, m, r):
        return jnp.broadcast_to(table[n, m, r : r + 1], (8, 128))

    def side(x, m):
        before = x[m - 1] if m else turn(x[3], 1)
        after = x[m + 1] if m < 3 else turn(x[0], 127)
        return before + after

    def diffract(source, begin, inner, orient, emit):
        rows, scaled = {}, {}

        def around(values, r, k, m):
            parts = [values[n][k][m] for n in (r - 1, r + 1) if n in values]
            if r in values:
                parts.append(side(values[r][k], m))
            return functools.reduce(lambda x, y: x + y, parts)

        def scale(r):
            out = []
            for k in range(2):
                new = []
                for m in range(4):
                    total = around(rows, r, k, m)
                    if r in rows:
                        total = total - 4.0 * rows[r][k][m]
                    new.append(spread(8, m, r) * total)
                out.append(new)
            scaled[r] = out

        def finish(r):
            for m in range(4):
                re, im = (around(scaled, r, k, m) for k in range(2))
                if r in rows:
                    re, im = rows[r][0][m] - re, rows[r][1][m] - im
                else:
                    re, im = -re, -im
                if r in scaled:
                    mre, mim = scaled[r][0][m], scaled[r][1][m]
                    turned = orient * ratio
                    re = re + (4.0 * mre - turned * mim)
                    im = im + (4.0 * mim + turned * mre)
                emit(r, m, re, im)

        def advance(r):
            if r - 1 >= begin + inner:
                scale(r - 1)
            if r - 2 >= begin + 2 * inner:
                finish(r - 2)

        def opposite(row):
            return [[turn(x, 64) for x in part] for part in row]

        for r in range(begin, 16):
            rows[r] = source(r)
            advance(r)
        rows[16] = opposite(rows[15])
        advance(16)
        scaled[16] = opposite(scaled[15])
        finish(15)

    def received(comp, k):
        parts = [
            got_ref[pl.ds(128 * n + 8 * comp + k, 8, stride=16), :] for n in range(4)
        ]
        out = []
        for m in range(4):
            x = parts[3]
            for n in range(3):
                x = jnp.where(group == (m + n) % 4, parts[n], x)
            if m:
                x = picked(x, half + 16 * jnp.bitwise_and(group + m, 3) + place)
            out.append(x)
        return out

    head = received(0, 0)
    corner = jnp.bitwise_and(lane, 48)
    row_turns = picked(head[0], corner)
    col_turns = picked(head[1], corner)
    row0 = (top + jnp.where(upper, 0, 31)).astype(jnp.float32)
    row_part = row_turns * row0 * (1.0 / 256.0)
    col_part = col_turns * columns(0).astype(jnp.float32) * (1.0 / 1024.0)
    row_part = row_part - jnp.floor(row_part)
    col_part = col_part - jnp.floor(col_part)

    def unit(t):
        return jnp.cos(t), jnp.sin(t)

    def times(a, b):
        return a[0] * b[0] - a[1] * b[1], a[0] * b[1] + a[1] * b[0]

    wave = [unit(two_pi * (row_part + col_part))]
    step = unit(two_pi / 256.0 * row_turns * jnp.where(upper, 1.0, -1.0))
    across = unit(two_pi / 1024.0 * col_turns)
    for _ in range(3):
        wave.append(times(wave[-1], across))
    waves = [wave]

    def from_wave(r):
        while len(waves) <= r:
            waves.append([times(x, step) for x in waves[-1]])
        return [[x[k] for x in waves[r]] for k in range(2)]

    def from_field(r):
        return [[field[k, r, m] for m in range(4)] for k in range(2)]

    def forward(layer):
        def source(r):
            re, im = from_wave(r) if layer == 0 else from_field(r)
            out = ([], [])
            for m in range(4):
                v = times((spread(2 * layer, m, r), spread(2 * layer + 1, m, r)), (re[m], im[m]))
                for k in range(2):
                    stored[2 * layer + k, r, m] = v[k]
                    out[k].append(v[k])
            return out

        measured_rows = {}

        def emit(r, m, re, im):
            if layer < 3:
                field[0, r, m], field[1, r, m] = re, im
                return
            if r not in measured_rows:
                measured_rows[r] = [received(k, r - 8) for k in range(2)]
            column = columns(m)
            keep = (column >= 0) & (column < 1024)
            field[0, r, m] = jnp.where(keep, re - measured_rows[r][0][m], 0.0)
            field[1, r, m] = jnp.where(keep, im - measured_rows[r][1][m], 0.0)

        diffract(source, 2 * layer, 1, 1.0, emit)

    def backward(layer):
        def emit(r, m, re, im):
            vre, vim = stored[2 * layer, r, m], stored[2 * layer + 1, r, m]
            for out, x in enumerate((vre * im - vim * re, vre * re + vim * im)):
                sums[2 * layer + out, m, r : r + 1] = jnp.sum(x, axis=0, keepdims=True)
            if layer:
                a, b = spread(2 * layer, m, r), spread(2 * layer + 1, m, r)
                field[0, r, m], field[1, r, m] = a * re + b * im, a * im - b * re

        diffract(from_field, 2 * layer + 2, -1, -1.0, emit)

    for layer in range(4):
        forward(layer)
        for n in range(2):
            for m in range(4):
                if layer:
                    sums[2 * layer + n, m, 0 : 2 * layer] = jnp.zeros((2 * layer, 128))
    for layer in (3, 2, 1, 0):
        backward(layer)

    source, target = square_iotas()
    near = (jnp.bitwise_and(source, 64) == jnp.bitwise_and(target, 64)) & (
        jnp.bitwise_and(source, 15) == jnp.bitwise_and(target, 63) // 4
    )
    total = None
    for m in range(4):
        x = sums[:, m].reshape(128, 128)
        x = permuted(x, near & (jnp.bitwise_and(target, 3) == m))
        total = x if total is None else total + x
    flat[...] = total

    def plain(n, q):
        return flat[16 * n + 8 * q : 16 * n + 8 * q + 8]

    blocks = [[None] * 4 for _ in range(2)]
    for pair in range(2):
        for q in range(2):
            for n in range(4):
                out, sl = divmod(n, 2)
                x = plain(2 * (2 * pair + sl) + out, q)
                x = -x if out else x
                for b, y in ((q, turn(x, 32 * n - 16)), (3 - q, turn(x, 32 * n - 80))):
                    old = blocks[pair][b]
                    blocks[pair][b] = y if old is None else jnp.where(lane < 32 * n, old, y)
        for b in (2, 3):
            blocks[pair][b] = flipped(blocks[pair][b])
    mine = [jnp.where(first, a, b) for a, b in zip(*blocks)]
    other = [jnp.where(first, b, a) for a, b in zip(*blocks)]
    none = jnp.zeros((8, 128), jnp.float32)
    for parts, ref in ((mine, mine_ref), (other, other_ref)):
        for b in range(4):
            ref[8 * b : 8 * b + 8] = jnp.where(
                first, parts[b + 1] if b < 3 else none, parts[b - 1] if b > 0 else none
            )
    for pair in range(2):
        edge_ref[pair] = jnp.where(first, blocks[pair][0], blocks[pair][3])


def add_edges(place_ref, other_ref, edge_ref, out_ref):
    first = place_ref[2] == 0
    edge = jnp.where(first, edge_ref[1], edge_ref[0])
    none = jnp.zeros((8, 128), jnp.float32)
    out_ref[0:8] = other_ref[0:8] + jnp.where(first, edge, none)
    out_ref[8:24] = other_ref[8:24]
    out_ref[24:32] = other_ref[24:32] + jnp.where(first, none, edge)


def combine(place_ref, mine_ref, other_ref, edge_ref, phase_ref, atten_ref):
    first = place_ref[2] == 0
    edge = jnp.where(first, edge_ref[0], edge_ref[1])
    for b in range(4):
        rows = slice(8 * b, 8 * b + 8)
        total = mine_ref[rows] + other_ref[rows]
        if b == 0:
            total = total + jnp.where(first, edge, 0.0)
        if b == 3:
            total = total + jnp.where(first, 0.0, edge)
        for sl in range(2):
            phase_ref[sl, rows] = turn(total, -32 * sl)[:, 0:32]
            atten_ref[sl, rows] = turn(total, -64 - 32 * sl)[:, 0:32]


def body(phase_delay, attenuation, measured, angles):
    block = lax.axis_index("illum")
    slab = lax.axis_index("slab")
    cut = lax.axis_index("cuts")
    place = jnp.stack([jnp.full((8, 128), n, jnp.int32) for n in (block, slab, cut)])
    n_slabs, n_blocks = lax.axis_size("slab"), lax.axis_size("illum")
    rows_axis = ("slab", "cuts")

    def both_ways(pairs):
        return pairs + [(b, a) for a, b in pairs]

    partner = both_ways([(2 * s, 2 * s + 1) for s in range(n_slabs)])
    across = both_ways([(2 * s + 1, 2 * s + 2) for s in range(n_slabs - 1)])
    beside = both_ways([(2 * i + 1, 2 * i + 2) for i in range(n_blocks - 1)])
    phase_delay, attenuation, measured, angles = (
        pltpu.with_memory_space_constraint(x, pltpu.HBM)
        for x in (phase_delay, attenuation, measured, angles)
    )
    mine, whole, head = pl.pallas_call(
        pack_object,
        out_shape=(f32(32, 128), f32(2, 32, 1024), f32(8, 128)),
        in_specs=[HBM] * 4,
        out_specs=(VMEM,) * 3,
        scratch_shapes=[
            pltpu.VMEM((2, 32, 32), jnp.float32),
            pltpu.VMEM((2, 32, 32), jnp.float32),
            pltpu.SMEM((1, 2), jnp.int32),
            pltpu.SemaphoreType.DMA((4,)),
        ],
        compiler_params=small,
    )(phase_delay, attenuation, measured, angles)
    other = lax.ppermute(mine, rows_axis, partner)
    sent = pl.pallas_call(
        pack_measured,
        out_shape=f32(32, 16, 128),
        in_specs=[VMEM] * 3,
        out_specs=HBM,
        scratch_shapes=[
            pltpu.VMEM((512, 128), jnp.float32),
            pltpu.VMEM((32, 16, 128), jnp.float32),
            pltpu.SemaphoreType.DMA((4,)),
        ],
        compiler_params=small,
    )(place, whole, head)
    near = pl.pallas_call(
        pack_sides,
        out_shape=f32(32, 128),
        in_specs=[VMEM] * 3,
        out_specs=VMEM,
        compiler_params=small,
    )(place, mine, other)
    near = lax.ppermute(near, ("illum", "cuts"), beside)
    got = lax.all_to_all(sent, "illum", 0, 0, tiled=True)
    far = lax.ppermute(near, rows_axis, partner)
    edges = pl.pallas_call(
        pack_edges,
        out_shape=f32(4, 8, 128),
        in_specs=[VMEM] * 5,
        out_specs=VMEM,
        compiler_params=small,
    )(place, mine, other, near, far)
    edges = lax.ppermute(edges, rows_axis, across)
    here, from_left, from_right = pl.pallas_call(
        pack_rows,
        out_shape=(f32(2, 32, 128), f32(32, 128), f32(32, 128)),
        in_specs=[VMEM] * 6,
        out_specs=(VMEM,) * 3,
        compiler_params=small,
    )(place, mine, other, near, far, edges)

    mine, other, edges = pl.pallas_call(
        march,
        out_shape=(f32(32, 128), f32(32, 128), f32(2, 8, 128)),
        in_specs=[VMEM] * 5,
        out_specs=(VMEM,) * 3,
        scratch_shapes=[
            pltpu.VMEM((9, 4, 16, 128), jnp.float32),
            pltpu.VMEM((128, 128), jnp.float32),
            pltpu.VMEM((2, 16, 4, 8, 128), jnp.float32),
            pltpu.VMEM((8, 16, 4, 8, 128), jnp.float32),
            pltpu.VMEM((8, 4, 16, 128), jnp.float32),
        ],
        compiler_params=large,
    )(place, here, from_left, from_right, got.reshape(512, 128))
    edges = lax.ppermute(edges, rows_axis, across)
    other = pl.pallas_call(
        add_edges,
        out_shape=f32(32, 128),
        in_specs=[VMEM] * 3,
        out_specs=VMEM,
        compiler_params=small,
    )(place, other, edges)
    other = lax.ppermute(other, rows_axis, partner)
    return pl.pallas_call(
        combine,
        out_shape=(f32(2, 32, 32), f32(2, 32, 32)),
        in_specs=[VMEM] * 4,
        out_specs=(VMEM, VMEM),
        compiler_params=small,
    )(place, mine, other, edges)


def solution(mesh):
    placed = (
        P("cuts", "slab", "illum"),
        P("cuts", "slab", "illum"),
        P("illum", None, "slab", None),
        P("illum", None),
    )
    return jax.shard_map(
        body,
        mesh=mesh,
        in_specs=placed,
        out_specs=(P("cuts", "slab", "illum"), P("cuts", "slab", "illum")),
        check_vma=False,
    )
```

```python
import functools
import math

import jax
import jax.numpy as jnp
from jax import lax
from jax.experimental import pallas as pl
from jax.experimental.pallas import tpu as pltpu
from jax.sharding import PartitionSpec as P


step_coeff = 0.08
square_coeff = 0.0032
ratio = step_coeff / square_coeff
two_pi = 2.0 * math.pi

HALO = 8
REACH = 16
VMEM = pl.BlockSpec(memory_space=pltpu.VMEM)
SMEM = pl.BlockSpec(memory_space=pltpu.SMEM)
HBM = pl.BlockSpec(memory_space=pltpu.HBM)
small = pltpu.CompilerParams(vmem_limit_bytes=1 << 20)
large = pltpu.CompilerParams(vmem_limit_bytes=8 << 20)


def f32(*shape):
    return jax.ShapeDtypeStruct(shape, jnp.float32)


def lanes_of(shape):
    return lax.broadcasted_iota(jnp.int32, shape, 1)


def turn(x, by):
    by %= 128
    return pltpu.roll(x, by, 1) if by else x


def pack_object(
    phase_ref, atten_ref, measured_ref, angles_ref,
    out_ref, whole_ref, head_ref,
    phase, atten, turns, sems,
):
    copies = [
        pltpu.make_async_copy(phase_ref, phase, sems.at[0]),
        pltpu.make_async_copy(atten_ref, atten, sems.at[1]),
        pltpu.make_async_copy(angles_ref, turns, sems.at[2]),
        pltpu.make_async_copy(measured_ref.at[0], whole_ref, sems.at[3]),
    ]
    for copy in copies:
        copy.start()
    for copy in copies[:3]:
        copy.wait()
    for n, (ref, layer) in enumerate(((phase, 0), (phase, 1), (atten, 0), (atten, 1))):
        out_ref[:, 32 * n : 32 * n + 32] = ref[layer]
    lane = lanes_of((8, 128))
    head_ref[...] = jnp.where(lane == 0, turns[0, 0], turns[0, 1]).astype(jnp.float32)
    copies[3].wait()


def pairs_of(first, mine_ref, other_ref, rows):
    mine, other = mine_ref[rows], other_ref[rows]
    return [jnp.where(first, mine, other), jnp.where(first, other, mine)]


def sides_of(first, near_ref, far_ref, rows):
    near, far = near_ref[rows], far_ref[rows]
    return [jnp.where(first, near, far), jnp.where(first, far, near)]


def pack_sides(place_ref, mine_ref, other_ref, out_ref):
    first = place_ref[2] == 0
    lane = lanes_of((8, 128))
    spots = 32 * jnp.bitwise_and(lane // 16, 3) + jnp.bitwise_and(lane, 15)
    for block in range(4):
        rows = slice(8 * block, 8 * block + 8)
        both = pairs_of(first, mine_ref, other_ref, rows)
        left, right = (
            jnp.where(lane < 64, *(picked(x, spots + shift) for x in both)) for shift in (0, 16)
        )
        out_ref[rows] = jnp.where(first, left, right)


def pack_edges(place_ref, mine_ref, other_ref, near_ref, across_ref, along_ref):
    first = place_ref[2] == 0
    top, bottom = (
        pairs_of(first, mine_ref, other_ref, rows) + [near_ref[rows]]
        for rows in (slice(0, 8), slice(24, 32))
    )
    for k in range(3):
        across_ref[k] = jnp.where(first, top[k], bottom[k])
    along_ref[...] = jnp.where(first, bottom[2], top[2])


def pack_rows(
    place_ref, mine_ref, other_ref, near_ref, far_ref, across_ref, along_ref,
    out_ref, left_ref, right_ref,
):
    first = place_ref[2] == 0
    near_edge, far_edge = along_ref[...], across_ref[2]
    edges = [
        across_ref[0],
        across_ref[1],
        jnp.where(first, near_edge, far_edge),
        jnp.where(first, far_edge, near_edge),
    ]
    blocks = []
    for block in range(4):
        rows = slice(8 * block, 8 * block + 8)
        blocks.append(
            pairs_of(first, mine_ref, other_ref, rows)
            + sides_of(first, near_ref, far_ref, rows)
        )
    for block in range(4):
        rows = slice(8 * block, 8 * block + 8)
        new = []
        for k in range(4):
            above = blocks[block - 1][k] if block else edges[k]
            below = blocks[block + 1][k] if block < 3 else edges[k]
            new.append(jnp.where(first, above, below))
        out_ref[0, rows], out_ref[1, rows], left_ref[rows], right_ref[rows] = new


def flipped(x):
    rows = 7 - lax.broadcasted_iota(jnp.int32, (8, 128), 0)
    return jnp.take_along_axis(x, rows, axis=0)


def picked(x, lanes):
    return jnp.take_along_axis(x, lanes, axis=1)


def thirds(x):
    parts = []
    for _ in range(3):
        part = x.astype(jnp.bfloat16)
        x = x - part.astype(jnp.float32)
        parts.append(part)
    return jnp.concatenate(parts, axis=1)


def permuted(x, chosen):
    ones = jnp.where(chosen, 1.0, 0.0).astype(jnp.bfloat16)
    return jnp.dot(
        thirds(x),
        jnp.concatenate([ones] * 3, axis=0),
        preferred_element_type=jnp.float32,
    )


def square_iotas(width=128):
    shape = (128, width)
    return lax.broadcasted_iota(jnp.int32, shape, 0), lanes_of(shape)


def pack_measured(place_ref, whole_ref, head_ref, out_ref, plain, packed, sems):
    lane = lanes_of((8, 128))
    head = head_ref[...]
    zero = jnp.zeros((8, 128), jnp.float32)
    source, target = square_iotas()
    m = jnp.bitwise_and(target // 16 - jnp.tile(place_ref[0] // 8, (16, 1)), 3)
    chosen = source == jnp.bitwise_and(target, 64) + 4 * jnp.bitwise_and(target, 15) + m
    cut = place_ref[2]
    regs = []
    for comp in range(2):
        rows = []
        for a in range(2):
            rows.append([])
            for n in range(8):
                at = slice(128 * n, 128 * n + 128)
                x = jnp.where(
                    cut == 0,
                    whole_ref[comp, 8 * a : 8 * a + 8, at],
                    whole_ref[comp, 8 * a + 16 : 8 * a + 24, at],
                )
                rows[a].append(flipped(x) if a else x)
        regs.append(rows)
    copies = []
    for j in range(32):
        v, r = divmod(32 * j - REACH, 128)
        for comp in range(2):
            parts = []
            for a in range(2):
                left = regs[comp][a][v] if v >= 0 else zero
                part = turn(left, 64 * a - r)
                if r > 64:
                    right = regs[comp][a][v + 1] if v + 1 < 8 else zero
                    part = jnp.where(lane - 64 * a < 128 - r, part, turn(right, 64 * a - r))
                parts.append(part)
            both = jnp.where(lane < 64, parts[0], parts[1])
            if comp == 0:
                both = jnp.where(lane < 2, head, both)
            plain[16 * j + 8 * comp : 16 * j + 8 * comp + 8] = both
        if j % 8 == 7:
            part = pl.ds(j - 7, 8)
            moved = permuted(plain[16 * j - 112 : 16 * j + 16], chosen)
            packed[part] = moved.reshape(8, 16, 128)
            copies.append(
                pltpu.make_async_copy(packed.at[part], out_ref.at[part], sems.at[j // 8])
            )
            copies[-1].start()
    for copy in copies:
        copy.wait()


def march(
    place_ref, here_ref, left_ref, right_ref, got_ref,
    mine_ref, other_ref, edge_ref,
    table, flat, field, stored, sums,
):
    block, slab, cut = place_ref[0], place_ref[1], place_ref[2]
    first = cut == 0
    lane = lanes_of((8, 128))
    sub = lax.broadcasted_iota(jnp.int32, (8, 128), 0)
    upper = lane < 64
    window = jnp.bitwise_and(lane, 63)
    half = jnp.bitwise_and(lane, 64)
    place = jnp.bitwise_and(lane, 15)
    group = jnp.bitwise_and(lane // 16, 3)
    top = 32 * slab + 16 * cut - HALO
    left_column = 32 * block - REACH

    def columns(m):
        return left_column + 4 * place + m

    for q in range(2):
        row = top + jnp.where(upper, 8 * q + sub, 31 - 8 * q - sub)
        row_inside = (row >= 0) & (row < 256)
        column = left_column + window
        inside = row_inside & (column >= 0) & (column < 1024)
        for m in range(4):
            column = columns(m)
            table[8, m, 8 * q : 8 * q + 8] = jnp.where(
                row_inside & (column >= 0) & (column < 1024), square_coeff, 0.0
            )
        for layer in range(4):
            pair, sl = divmod(layer, 2)
            values = []
            for n in (sl, 2 + sl):
                halves = []
                for a, b in ((0, q), (1, 3 - q)):
                    rows = slice(8 * b, 8 * b + 8)
                    at = 64 * (a - pair) - 16 * n
                    halves.append(
                        jnp.where(
                            window < 16,
                            turn(left_ref[rows], at),
                            jnp.where(
                                window < 48,
                                turn(here_ref[pair, rows], 64 * a - 32 * n + 16),
                                turn(right_ref[rows], at + 48),
                            ),
                        )
                    )
                values.append(jnp.where(upper, halves[0], flipped(halves[1])))
            damping = jnp.where(inside, jnp.exp(-values[1]), 0.0)
            re, im = damping * jnp.cos(values[0]), damping * jnp.sin(values[0])
            flat[32 * layer + 8 * q : 32 * layer + 8 * q + 8] = re
            flat[32 * layer + 8 * q + 16 : 32 * layer + 8 * q + 24] = im
    source, target = square_iotas(512)
    spot = jnp.bitwise_and(target, 64) + 4 * jnp.bitwise_and(target, 15) + target // 128
    wide = permuted(flat[...], source == spot)
    for m in range(4):
        table[0:8, m] = wide[:, 128 * m : 128 * m + 128].reshape(8, 16, 128)

    def spread(n, m, r):
        return jnp.broadcast_to(table[n, m, r : r + 1], (8, 128))

    def side(x, m):
        before = x[m - 1] if m else turn(x[3], 1)
        after = x[m + 1] if m < 3 else turn(x[0], 127)
        return before + after

    def diffract(source, begin, inner, orient, emit):
        rows, scaled = {}, {}

        def around(values, r, k, m):
            parts = [values[n][k][m] for n in (r - 1, r + 1) if n in values]
            if r in values:
                parts.append(side(values[r][k], m))
            return functools.reduce(lambda x, y: x + y, parts)

        def scale(r):
            out = []
            for k in range(2):
                new = []
                for m in range(4):
                    total = around(rows, r, k, m)
                    if r in rows:
                        total = total - 4.0 * rows[r][k][m]
                    new.append(spread(8, m, r) * total)
                out.append(new)
            scaled[r] = out

        def finish(r):
            for m in range(4):
                re, im = (around(scaled, r, k, m) for k in range(2))
                if r in rows:
                    re, im = rows[r][0][m] - re, rows[r][1][m] - im
                else:
                    re, im = -re, -im
                if r in scaled:
                    mre, mim = scaled[r][0][m], scaled[r][1][m]
                    turned = orient * ratio
                    re = re + (4.0 * mre - turned * mim)
                    im = im + (4.0 * mim + turned * mre)
                emit(r, m, re, im)

        def advance(r):
            if r - 1 >= begin + inner:
                scale(r - 1)
            if r - 2 >= begin + 2 * inner:
                finish(r - 2)

        def opposite(row):
            return [[turn(x, 64) for x in part] for part in row]

        for r in range(begin, 16):
            rows[r] = source(r)
            advance(r)
        rows[16] = opposite(rows[15])
        advance(16)
        scaled[16] = opposite(scaled[15])
        finish(15)

    def received(comp, k):
        parts = [
            got_ref[pl.ds(128 * n + 8 * comp + k, 8, stride=16), :] for n in range(4)
        ]
        out = []
        for m in range(4):
            x = parts[3]
            for n in range(3):
                x = jnp.where(group == (m + n) % 4, parts[n], x)
            if m:
                x = picked(x, half + 16 * jnp.bitwise_and(group + m, 3) + place)
            out.append(x)
        return out

    head = received(0, 0)
    corner = jnp.bitwise_and(lane, 48)
    row_turns = picked(head[0], corner)
    col_turns = picked(head[1], corner)
    row0 = (top + jnp.where(upper, 0, 31)).astype(jnp.float32)
    row_part = row_turns * row0 * (1.0 / 256.0)
    col_part = col_turns * columns(0).astype(jnp.float32) * (1.0 / 1024.0)
    row_part = row_part - jnp.floor(row_part)
    col_part = col_part - jnp.floor(col_part)

    def unit(t):
        return jnp.cos(t), jnp.sin(t)

    def times(a, b):
        return a[0] * b[0] - a[1] * b[1], a[0] * b[1] + a[1] * b[0]

    wave = [unit(two_pi * (row_part + col_part))]
    step = unit(two_pi / 256.0 * row_turns * jnp.where(upper, 1.0, -1.0))
    across = unit(two_pi / 1024.0 * col_turns)
    for _ in range(3):
        wave.append(times(wave[-1], across))
    waves = [wave]

    def from_wave(r):
        while len(waves) <= r:
            waves.append([times(x, step) for x in waves[-1]])
        return [[x[k] for x in waves[r]] for k in range(2)]

    def from_field(r):
        return [[field[k, r, m] for m in range(4)] for k in range(2)]

    def forward(layer):
        def source(r):
            re, im = from_wave(r) if layer == 0 else from_field(r)
            out = ([], [])
            for m in range(4):
                v = times((spread(2 * layer, m, r), spread(2 * layer + 1, m, r)), (re[m], im[m]))
                for k in range(2):
                    stored[2 * layer + k, r, m] = v[k]
                    out[k].append(v[k])
            return out

        measured_rows = {}

        def emit(r, m, re, im):
            if layer < 3:
                field[0, r, m], field[1, r, m] = re, im
                return
            if r not in measured_rows:
                measured_rows[r] = [received(k, r - 8) for k in range(2)]
            column = columns(m)
            keep = (column >= 0) & (column < 1024)
            field[0, r, m] = jnp.where(keep, re - measured_rows[r][0][m], 0.0)
            field[1, r, m] = jnp.where(keep, im - measured_rows[r][1][m], 0.0)

        diffract(source, 2 * layer, 1, 1.0, emit)

    def backward(layer):
        def emit(r, m, re, im):
            vre, vim = stored[2 * layer, r, m], stored[2 * layer + 1, r, m]
            for out, x in enumerate((vre * im - vim * re, vre * re + vim * im)):
                sums[2 * layer + out, m, r : r + 1] = jnp.sum(x, axis=0, keepdims=True)
            if layer:
                a, b = spread(2 * layer, m, r), spread(2 * layer + 1, m, r)
                field[0, r, m], field[1, r, m] = a * re + b * im, a * im - b * re

        diffract(from_field, 2 * layer + 2, -1, -1.0, emit)

    for layer in range(4):
        forward(layer)
        for n in range(2):
            for m in range(4):
                if layer:
                    sums[2 * layer + n, m, 0 : 2 * layer] = jnp.zeros((2 * layer, 128))
    for layer in (3, 2, 1, 0):
        backward(layer)

    source, target = square_iotas()
    near = (jnp.bitwise_and(source, 64) == jnp.bitwise_and(target, 64)) & (
        jnp.bitwise_and(source, 15) == jnp.bitwise_and(target, 63) // 4
    )
    total = None
    for m in range(4):
        x = sums[:, m].reshape(128, 128)
        x = permuted(x, near & (jnp.bitwise_and(target, 3) == m))
        total = x if total is None else total + x
    flat[...] = total

    def plain(n, q):
        return flat[16 * n + 8 * q : 16 * n + 8 * q + 8]

    blocks = [[None] * 4 for _ in range(2)]
    for pair in range(2):
        for q in range(2):
            for n in range(4):
                out, sl = divmod(n, 2)
                x = plain(2 * (2 * pair + sl) + out, q)
                x = -x if out else x
                for b, y in ((q, turn(x, 32 * n - 16)), (3 - q, turn(x, 32 * n - 80))):
                    old = blocks[pair][b]
                    blocks[pair][b] = y if old is None else jnp.where(lane < 32 * n, old, y)
        for b in (2, 3):
            blocks[pair][b] = flipped(blocks[pair][b])
    mine = [jnp.where(first, a, b) for a, b in zip(*blocks)]
    other = [jnp.where(first, b, a) for a, b in zip(*blocks)]
    none = jnp.zeros((8, 128), jnp.float32)
    for parts, ref in ((mine, mine_ref), (other, other_ref)):
        for b in range(4):
            ref[8 * b : 8 * b + 8] = jnp.where(
                first, parts[b + 1] if b < 3 else none, parts[b - 1] if b > 0 else none
            )
    for pair in range(2):
        edge_ref[pair] = jnp.where(first, blocks[pair][0], blocks[pair][3])


def add_edges(place_ref, other_ref, edge_ref, out_ref):
    first = place_ref[2] == 0
    edge = jnp.where(first, edge_ref[1], edge_ref[0])
    none = jnp.zeros((8, 128), jnp.float32)
    out_ref[0:8] = other_ref[0:8] + jnp.where(first, edge, none)
    out_ref[8:24] = other_ref[8:24]
    out_ref[24:32] = other_ref[24:32] + jnp.where(first, none, edge)


def combine(place_ref, mine_ref, other_ref, edge_ref, phase_ref, atten_ref):
    first = place_ref[2] == 0
    edge = jnp.where(first, edge_ref[0], edge_ref[1])
    for b in range(4):
        rows = slice(8 * b, 8 * b + 8)
        total = mine_ref[rows] + other_ref[rows]
        if b == 0:
            total = total + jnp.where(first, edge, 0.0)
        if b == 3:
            total = total + jnp.where(first, 0.0, edge)
        for sl in range(2):
            phase_ref[sl, rows] = turn(total, -32 * sl)[:, 0:32]
            atten_ref[sl, rows] = turn(total, -64 - 32 * sl)[:, 0:32]


def body(phase_delay, attenuation, measured, angles):
    block = lax.axis_index("illum")
    slab = lax.axis_index("slab")
    cut = lax.axis_index("cuts")
    place = jnp.stack([jnp.full((8, 128), n, jnp.int32) for n in (block, slab, cut)])
    n_slabs, n_blocks = lax.axis_size("slab"), lax.axis_size("illum")
    rows_axis = ("slab", "cuts")

    def both_ways(pairs):
        return pairs + [(b, a) for a, b in pairs]

    partner = both_ways([(2 * s, 2 * s + 1) for s in range(n_slabs)])
    across = both_ways([(2 * s + 1, 2 * s + 2) for s in range(n_slabs - 1)])
    along = [(2 * s, 2 * s + 2) for s in range(n_slabs - 1)]
    along += [(2 * s + 3, 2 * s + 1) for s in range(n_slabs - 1)]
    beside = both_ways([(2 * i + 1, 2 * i + 2) for i in range(n_blocks - 1)])
    phase_delay, attenuation, measured, angles = (
        pltpu.with_memory_space_constraint(x, pltpu.HBM)
        for x in (phase_delay, attenuation, measured, angles)
    )
    mine, whole, head = pl.pallas_call(
        pack_object,
        out_shape=(f32(32, 128), f32(2, 32, 1024), f32(8, 128)),
        in_specs=[HBM] * 4,
        out_specs=(VMEM,) * 3,
        scratch_shapes=[
            pltpu.VMEM((2, 32, 32), jnp.float32),
            pltpu.VMEM((2, 32, 32), jnp.float32),
            pltpu.SMEM((1, 2), jnp.int32),
            pltpu.SemaphoreType.DMA((4,)),
        ],
        compiler_params=small,
    )(phase_delay, attenuation, measured, angles)
    other = lax.ppermute(mine, rows_axis, partner)
    sent = pl.pallas_call(
        pack_measured,
        out_shape=f32(32, 16, 128),
        in_specs=[VMEM] * 3,
        out_specs=HBM,
        scratch_shapes=[
            pltpu.VMEM((512, 128), jnp.float32),
            pltpu.VMEM((32, 16, 128), jnp.float32),
            pltpu.SemaphoreType.DMA((4,)),
        ],
        compiler_params=small,
    )(place, whole, head)
    near = pl.pallas_call(
        pack_sides,
        out_shape=f32(32, 128),
        in_specs=[VMEM] * 3,
        out_specs=VMEM,
        compiler_params=small,
    )(place, mine, other)
    near = lax.ppermute(near, ("illum", "cuts"), beside)
    got = lax.all_to_all(sent, "illum", 0, 0, tiled=True)
    far = lax.ppermute(near, rows_axis, partner)
    across_part, along_part = pl.pallas_call(
        pack_edges,
        out_shape=(f32(3, 8, 128), f32(8, 128)),
        in_specs=[VMEM] * 4,
        out_specs=(VMEM,) * 2,
        compiler_params=small,
    )(place, mine, other, near)
    across_part = lax.ppermute(across_part, rows_axis, across)
    along_part = lax.ppermute(along_part, rows_axis, along)
    here, from_left, from_right = pl.pallas_call(
        pack_rows,
        out_shape=(f32(2, 32, 128), f32(32, 128), f32(32, 128)),
        in_specs=[VMEM] * 7,
        out_specs=(VMEM,) * 3,
        compiler_params=small,
    )(place, mine, other, near, far, across_part, along_part)

    mine, other, edges = pl.pallas_call(
        march,
        out_shape=(f32(32, 128), f32(32, 128), f32(2, 8, 128)),
        in_specs=[VMEM] * 5,
        out_specs=(VMEM,) * 3,
        scratch_shapes=[
            pltpu.VMEM((9, 4, 16, 128), jnp.float32),
            pltpu.VMEM((128, 128), jnp.float32),
            pltpu.VMEM((2, 16, 4, 8, 128), jnp.float32),
            pltpu.VMEM((8, 16, 4, 8, 128), jnp.float32),
            pltpu.VMEM((8, 4, 16, 128), jnp.float32),
        ],
        compiler_params=large,
    )(place, here, from_left, from_right, got.reshape(512, 128))
    edges = lax.ppermute(edges, rows_axis, across)
    other = pl.pallas_call(
        add_edges,
        out_shape=f32(32, 128),
        in_specs=[VMEM] * 3,
        out_specs=VMEM,
        compiler_params=small,
    )(place, other, edges)
    other = lax.ppermute(other, rows_axis, partner)
    return pl.pallas_call(
        combine,
        out_shape=(f32(2, 32, 32), f32(2, 32, 32)),
        in_specs=[VMEM] * 4,
        out_specs=(VMEM, VMEM),
        compiler_params=small,
    )(place, mine, other, edges)


def solution(mesh):
    placed = (
        P("cuts", "slab", "illum"),
        P("cuts", "slab", "illum"),
        P("illum", None, "slab", None),
        P("illum", None),
    )
    return jax.shard_map(
        body,
        mesh=mesh,
        in_specs=placed,
        out_specs=(P("cuts", "slab", "illum"), P("cuts", "slab", "illum")),
        check_vma=False,
    )
```

```python
import functools
import math

import jax
import jax.numpy as jnp
from jax import lax
from jax.experimental import pallas as pl
from jax.experimental.pallas import tpu as pltpu
from jax.sharding import PartitionSpec as P


step_coeff = 0.08
square_coeff = 0.0032
ratio = step_coeff / square_coeff
two_pi = 2.0 * math.pi

HALO = 8
REACH = 16
VMEM = pl.BlockSpec(memory_space=pltpu.VMEM)
SMEM = pl.BlockSpec(memory_space=pltpu.SMEM)
HBM = pl.BlockSpec(memory_space=pltpu.HBM)
small = pltpu.CompilerParams(vmem_limit_bytes=1 << 20)
large = pltpu.CompilerParams(vmem_limit_bytes=8 << 20)


def f32(*shape):
    return jax.ShapeDtypeStruct(shape, jnp.float32)


def lanes_of(shape):
    return lax.broadcasted_iota(jnp.int32, shape, 1)


def turn(x, by):
    by %= 128
    return pltpu.roll(x, by, 1) if by else x


def pack_object(
    phase_ref, atten_ref, measured_ref, angles_ref,
    out_ref, whole_ref, head_ref,
    phase, atten, turns, sems,
):
    copies = [
        pltpu.make_async_copy(phase_ref, phase, sems.at[0]),
        pltpu.make_async_copy(atten_ref, atten, sems.at[1]),
        pltpu.make_async_copy(angles_ref, turns, sems.at[2]),
        pltpu.make_async_copy(measured_ref.at[0], whole_ref, sems.at[3]),
    ]
    for copy in copies:
        copy.start()
    for copy in copies[:3]:
        copy.wait()
    for n, (ref, layer) in enumerate(((phase, 0), (phase, 1), (atten, 0), (atten, 1))):
        out_ref[:, 32 * n : 32 * n + 32] = ref[layer]
    lane = lanes_of((8, 128))
    head_ref[...] = jnp.where(lane == 0, turns[0, 0], turns[0, 1]).astype(jnp.float32)
    copies[3].wait()


def pairs_of(first, mine_ref, other_ref, rows):
    mine, other = mine_ref[rows], other_ref[rows]
    return [jnp.where(first, mine, other), jnp.where(first, other, mine)]


def sides_of(first, near_ref, far_ref, rows):
    near, far = near_ref[rows], far_ref[rows]
    return [jnp.where(first, near, far), jnp.where(first, far, near)]


def pack_sides(place_ref, mine_ref, other_ref, out_ref):
    first = place_ref[2] == 0
    lane = lanes_of((8, 128))
    spots = 32 * jnp.bitwise_and(lane // 16, 3) + jnp.bitwise_and(lane, 15)
    for block in range(4):
        rows = slice(8 * block, 8 * block + 8)
        both = pairs_of(first, mine_ref, other_ref, rows)
        left, right = (
            jnp.where(lane < 64, *(picked(x, spots + shift) for x in both)) for shift in (0, 16)
        )
        out_ref[rows] = jnp.where(first, left, right)


def pack_edges(place_ref, mine_ref, other_ref, near_ref, across_ref, along_ref):
    first = place_ref[2] == 0
    top, bottom = (
        pairs_of(first, mine_ref, other_ref, rows) + [near_ref[rows]]
        for rows in (slice(0, 8), slice(24, 32))
    )
    for k in range(3):
        across_ref[k] = jnp.where(first, top[k], bottom[k])
    along_ref[...] = jnp.where(first, bottom[2], top[2])


def pack_rows(
    place_ref, mine_ref, other_ref, near_ref, far_ref, across_ref, along_ref,
    out_ref, left_ref, right_ref,
):
    first = place_ref[2] == 0
    near_edge, far_edge = along_ref[...], across_ref[2]
    edges = [
        across_ref[0],
        across_ref[1],
        jnp.where(first, near_edge, far_edge),
        jnp.where(first, far_edge, near_edge),
    ]
    blocks = []
    for block in range(4):
        rows = slice(8 * block, 8 * block + 8)
        blocks.append(
            pairs_of(first, mine_ref, other_ref, rows)
            + sides_of(first, near_ref, far_ref, rows)
        )
    for block in range(4):
        rows = slice(8 * block, 8 * block + 8)
        new = []
        for k in range(4):
            above = blocks[block - 1][k] if block else edges[k]
            below = blocks[block + 1][k] if block < 3 else edges[k]
            new.append(jnp.where(first, above, below))
        out_ref[0, rows], out_ref[1, rows], left_ref[rows], right_ref[rows] = new


def flipped(x):
    rows = 7 - lax.broadcasted_iota(jnp.int32, (8, 128), 0)
    return jnp.take_along_axis(x, rows, axis=0)


def picked(x, lanes):
    return jnp.take_along_axis(x, lanes, axis=1)


def thirds(x):
    parts = []
    for _ in range(3):
        part = x.astype(jnp.bfloat16)
        x = x - part.astype(jnp.float32)
        parts.append(part)
    return jnp.concatenate(parts, axis=1)


def permuted(x, chosen):
    ones = jnp.where(chosen, 1.0, 0.0).astype(jnp.bfloat16)
    return jnp.dot(
        thirds(x),
        jnp.concatenate([ones] * 3, axis=0),
        preferred_element_type=jnp.float32,
    )


def square_iotas(width=128):
    shape = (128, width)
    return lax.broadcasted_iota(jnp.int32, shape, 0), lanes_of(shape)


def pack_measured(place_ref, whole_ref, head_ref, out_ref, plain, packed, sems):
    lane = lanes_of((8, 128))
    head = head_ref[...]
    zero = jnp.zeros((8, 128), jnp.float32)
    source, target = square_iotas()
    m = jnp.bitwise_and(target // 16 - jnp.tile(place_ref[0] // 8, (16, 1)), 3)
    chosen = source == jnp.bitwise_and(target, 64) + 4 * jnp.bitwise_and(target, 15) + m
    cut = place_ref[2]
    regs = []
    for comp in range(2):
        rows = []
        for a in range(2):
            rows.append([])
            for n in range(8):
                at = slice(128 * n, 128 * n + 128)
                x = jnp.where(
                    cut == 0,
                    whole_ref[comp, 8 * a : 8 * a + 8, at],
                    whole_ref[comp, 8 * a + 16 : 8 * a + 24, at],
                )
                rows[a].append(flipped(x) if a else x)
        regs.append(rows)
    copies = []
    for j in range(32):
        v, r = divmod(32 * j - REACH, 128)
        for comp in range(2):
            parts = []
            for a in range(2):
                left = regs[comp][a][v] if v >= 0 else zero
                part = turn(left, 64 * a - r)
                if r > 64:
                    right = regs[comp][a][v + 1] if v + 1 < 8 else zero
                    part = jnp.where(lane - 64 * a < 128 - r, part, turn(right, 64 * a - r))
                parts.append(part)
            both = jnp.where(lane < 64, parts[0], parts[1])
            if comp == 0:
                both = jnp.where(lane < 2, head, both)
            plain[16 * j + 8 * comp : 16 * j + 8 * comp + 8] = both
        if j % 8 == 7:
            part = pl.ds(j - 7, 8)
            moved = permuted(plain[16 * j - 112 : 16 * j + 16], chosen)
            packed[part] = moved.reshape(8, 16, 128)
            copies.append(
                pltpu.make_async_copy(packed.at[part], out_ref.at[part], sems.at[j // 8])
            )
            copies[-1].start()
    for copy in copies:
        copy.wait()


def transmit(place_ref, here_ref, left_ref, right_ref, table, flat):
    sub = lax.broadcasted_iota(jnp.int32, (8, 128), 0)
    block, slab, cut = place_ref[0], place_ref[1], place_ref[2]
    lane = lanes_of((8, 128))
    upper = lane < 64
    window = jnp.bitwise_and(lane, 63)
    place = jnp.bitwise_and(lane, 15)
    top = 32 * slab + 16 * cut - HALO
    left_column = 32 * block - REACH

    def columns(m):
        return left_column + 4 * place + m

    for q in range(2):
        row = top + jnp.where(upper, 8 * q + sub, 31 - 8 * q - sub)
        row_inside = (row >= 0) & (row < 256)
        column = left_column + window
        inside = row_inside & (column >= 0) & (column < 1024)
        for m in range(4):
            column = columns(m)
            table[8, m, 8 * q : 8 * q + 8] = jnp.where(
                row_inside & (column >= 0) & (column < 1024), square_coeff, 0.0
            )
        for layer in range(4):
            pair, sl = divmod(layer, 2)
            values = []
            for n in (sl, 2 + sl):
                halves = []
                for a, b in ((0, q), (1, 3 - q)):
                    rows = slice(8 * b, 8 * b + 8)
                    at = 64 * (a - pair) - 16 * n
                    halves.append(
                        jnp.where(
                            window < 16,
                            turn(left_ref[rows], at),
                            jnp.where(
                                window < 48,
                                turn(here_ref[pair, rows], 64 * a - 32 * n + 16),
                                turn(right_ref[rows], at + 48),
                            ),
                        )
                    )
                values.append(jnp.where(upper, halves[0], flipped(halves[1])))
            damping = jnp.where(inside, jnp.exp(-values[1]), 0.0)
            re, im = damping * jnp.cos(values[0]), damping * jnp.sin(values[0])
            flat[32 * layer + 8 * q : 32 * layer + 8 * q + 8] = re
            flat[32 * layer + 8 * q + 16 : 32 * layer + 8 * q + 24] = im
    source, target = square_iotas(512)
    spot = jnp.bitwise_and(target, 64) + 4 * jnp.bitwise_and(target, 15) + target // 128
    wide = permuted(flat[...], source == spot)
    for m in range(4):
        table[0:8, m] = wide[:, 128 * m : 128 * m + 128].reshape(8, 16, 128)


def march(
    place_ref, table, got_ref,
    mine_ref, other_ref, edge_ref,
    flat, field, stored, sums,
):
    block, slab, cut = place_ref[0], place_ref[1], place_ref[2]
    first = cut == 0
    lane = lanes_of((8, 128))
    upper = lane < 64
    window = jnp.bitwise_and(lane, 63)
    half = jnp.bitwise_and(lane, 64)
    place = jnp.bitwise_and(lane, 15)
    group = jnp.bitwise_and(lane // 16, 3)
    top = 32 * slab + 16 * cut - HALO
    left_column = 32 * block - REACH

    def columns(m):
        return left_column + 4 * place + m

    def spread(n, m, r):
        return jnp.broadcast_to(table[n, m, r : r + 1], (8, 128))

    def side(x, m):
        before = x[m - 1] if m else turn(x[3], 1)
        after = x[m + 1] if m < 3 else turn(x[0], 127)
        return before + after

    def diffract(source, begin, inner, orient, emit):
        rows, scaled = {}, {}

        def around(values, r, k, m):
            parts = [values[n][k][m] for n in (r - 1, r + 1) if n in values]
            if r in values:
                parts.append(side(values[r][k], m))
            return functools.reduce(lambda x, y: x + y, parts)

        def scale(r):
            out = []
            for k in range(2):
                new = []
                for m in range(4):
                    total = around(rows, r, k, m)
                    if r in rows:
                        total = total - 4.0 * rows[r][k][m]
                    new.append(spread(8, m, r) * total)
                out.append(new)
            scaled[r] = out

        def finish(r):
            for m in range(4):
                re, im = (around(scaled, r, k, m) for k in range(2))
                if r in rows:
                    re, im = rows[r][0][m] - re, rows[r][1][m] - im
                else:
                    re, im = -re, -im
                if r in scaled:
                    mre, mim = scaled[r][0][m], scaled[r][1][m]
                    turned = orient * ratio
                    re = re + (4.0 * mre - turned * mim)
                    im = im + (4.0 * mim + turned * mre)
                emit(r, m, re, im)

        def advance(r):
            if r - 1 >= begin + inner:
                scale(r - 1)
            if r - 2 >= begin + 2 * inner:
                finish(r - 2)

        def opposite(row):
            return [[turn(x, 64) for x in part] for part in row]

        for r in range(begin, 16):
            rows[r] = source(r)
            advance(r)
        rows[16] = opposite(rows[15])
        advance(16)
        scaled[16] = opposite(scaled[15])
        finish(15)

    def received(comp, k):
        parts = [
            got_ref[pl.ds(128 * n + 8 * comp + k, 8, stride=16), :] for n in range(4)
        ]
        out = []
        for m in range(4):
            x = parts[3]
            for n in range(3):
                x = jnp.where(group == (m + n) % 4, parts[n], x)
            if m:
                x = picked(x, half + 16 * jnp.bitwise_and(group + m, 3) + place)
            out.append(x)
        return out

    head = received(0, 0)
    corner = jnp.bitwise_and(lane, 48)
    row_turns = picked(head[0], corner)
    col_turns = picked(head[1], corner)
    row0 = (top + jnp.where(upper, 0, 31)).astype(jnp.float32)
    row_part = row_turns * row0 * (1.0 / 256.0)
    col_part = col_turns * columns(0).astype(jnp.float32) * (1.0 / 1024.0)
    row_part = row_part - jnp.floor(row_part)
    col_part = col_part - jnp.floor(col_part)

    def unit(t):
        return jnp.cos(t), jnp.sin(t)

    def times(a, b):
        return a[0] * b[0] - a[1] * b[1], a[0] * b[1] + a[1] * b[0]

    wave = [unit(two_pi * (row_part + col_part))]
    step = unit(two_pi / 256.0 * row_turns * jnp.where(upper, 1.0, -1.0))
    across = unit(two_pi / 1024.0 * col_turns)
    for _ in range(3):
        wave.append(times(wave[-1], across))
    waves = [wave]

    def from_wave(r):
        while len(waves) <= r:
            waves.append([times(x, step) for x in waves[-1]])
        return [[x[k] for x in waves[r]] for k in range(2)]

    def from_field(r):
        return [[field[k, r, m] for m in range(4)] for k in range(2)]

    def forward(layer):
        def source(r):
            re, im = from_wave(r) if layer == 0 else from_field(r)
            out = ([], [])
            for m in range(4):
                v = times((spread(2 * layer, m, r), spread(2 * layer + 1, m, r)), (re[m], im[m]))
                for k in range(2):
                    stored[2 * layer + k, r, m] = v[k]
                    out[k].append(v[k])
            return out

        measured_rows = {}

        def emit(r, m, re, im):
            if layer < 3:
                field[0, r, m], field[1, r, m] = re, im
                return
            if r not in measured_rows:
                measured_rows[r] = [received(k, r - 8) for k in range(2)]
            column = columns(m)
            keep = (column >= 0) & (column < 1024)
            field[0, r, m] = jnp.where(keep, re - measured_rows[r][0][m], 0.0)
            field[1, r, m] = jnp.where(keep, im - measured_rows[r][1][m], 0.0)

        diffract(source, 2 * layer, 1, 1.0, emit)

    def backward(layer):
        def emit(r, m, re, im):
            vre, vim = stored[2 * layer, r, m], stored[2 * layer + 1, r, m]
            for out, x in enumerate((vre * im - vim * re, vre * re + vim * im)):
                sums[2 * layer + out, m, r : r + 1] = jnp.sum(x, axis=0, keepdims=True)
            if layer:
                a, b = spread(2 * layer, m, r), spread(2 * layer + 1, m, r)
                field[0, r, m], field[1, r, m] = a * re + b * im, a * im - b * re

        diffract(from_field, 2 * layer + 2, -1, -1.0, emit)

    for layer in range(4):
        forward(layer)
        for n in range(2):
            for m in range(4):
                if layer:
                    sums[2 * layer + n, m, 0 : 2 * layer] = jnp.zeros((2 * layer, 128))
    for layer in (3, 2, 1, 0):
        backward(layer)

    source, target = square_iotas()
    near = (jnp.bitwise_and(source, 64) == jnp.bitwise_and(target, 64)) & (
        jnp.bitwise_and(source, 15) == jnp.bitwise_and(target, 63) // 4
    )
    total = None
    for m in range(4):
        x = sums[:, m].reshape(128, 128)
        x = permuted(x, near & (jnp.bitwise_and(target, 3) == m))
        total = x if total is None else total + x
    flat[...] = total

    def plain(n, q):
        return flat[16 * n + 8 * q : 16 * n + 8 * q + 8]

    blocks = [[None] * 4 for _ in range(2)]
    for pair in range(2):
        for q in range(2):
            for n in range(4):
                out, sl = divmod(n, 2)
                x = plain(2 * (2 * pair + sl) + out, q)
                x = -x if out else x
                for b, y in ((q, turn(x, 32 * n - 16)), (3 - q, turn(x, 32 * n - 80))):
                    old = blocks[pair][b]
                    blocks[pair][b] = y if old is None else jnp.where(lane < 32 * n, old, y)
        for b in (2, 3):
            blocks[pair][b] = flipped(blocks[pair][b])
    mine = [jnp.where(first, a, b) for a, b in zip(*blocks)]
    other = [jnp.where(first, b, a) for a, b in zip(*blocks)]
    none = jnp.zeros((8, 128), jnp.float32)
    for parts, ref in ((mine, mine_ref), (other, other_ref)):
        for b in range(4):
            ref[8 * b : 8 * b + 8] = jnp.where(
                first, parts[b + 1] if b < 3 else none, parts[b - 1] if b > 0 else none
            )
    for pair in range(2):
        edge_ref[pair] = jnp.where(first, blocks[pair][0], blocks[pair][3])


def add_edges(place_ref, other_ref, edge_ref, out_ref):
    first = place_ref[2] == 0
    edge = jnp.where(first, edge_ref[1], edge_ref[0])
    none = jnp.zeros((8, 128), jnp.float32)
    out_ref[0:8] = other_ref[0:8] + jnp.where(first, edge, none)
    out_ref[8:24] = other_ref[8:24]
    out_ref[24:32] = other_ref[24:32] + jnp.where(first, none, edge)


def combine(place_ref, mine_ref, other_ref, edge_ref, phase_ref, atten_ref):
    first = place_ref[2] == 0
    edge = jnp.where(first, edge_ref[0], edge_ref[1])
    for b in range(4):
        rows = slice(8 * b, 8 * b + 8)
        total = mine_ref[rows] + other_ref[rows]
        if b == 0:
            total = total + jnp.where(first, edge, 0.0)
        if b == 3:
            total = total + jnp.where(first, 0.0, edge)
        for sl in range(2):
            phase_ref[sl, rows] = turn(total, -32 * sl)[:, 0:32]
            atten_ref[sl, rows] = turn(total, -64 - 32 * sl)[:, 0:32]


def body(phase_delay, attenuation, measured, angles):
    block = lax.axis_index("illum")
    slab = lax.axis_index("slab")
    cut = lax.axis_index("cuts")
    place = jnp.stack([jnp.full((8, 128), n, jnp.int32) for n in (block, slab, cut)])
    n_slabs, n_blocks = lax.axis_size("slab"), lax.axis_size("illum")
    rows_axis = ("slab", "cuts")

    def both_ways(pairs):
        return pairs + [(b, a) for a, b in pairs]

    partner = both_ways([(2 * s, 2 * s + 1) for s in range(n_slabs)])
    across = both_ways([(2 * s + 1, 2 * s + 2) for s in range(n_slabs - 1)])
    along = [(2 * s, 2 * s + 2) for s in range(n_slabs - 1)]
    along += [(2 * s + 3, 2 * s + 1) for s in range(n_slabs - 1)]
    beside = both_ways([(2 * i + 1, 2 * i + 2) for i in range(n_blocks - 1)])
    phase_delay, attenuation, measured, angles = (
        pltpu.with_memory_space_constraint(x, pltpu.HBM)
        for x in (phase_delay, attenuation, measured, angles)
    )
    mine, whole, head = pl.pallas_call(
        pack_object,
        out_shape=(f32(32, 128), f32(2, 32, 1024), f32(8, 128)),
        in_specs=[HBM] * 4,
        out_specs=(VMEM,) * 3,
        scratch_shapes=[
            pltpu.VMEM((2, 32, 32), jnp.float32),
            pltpu.VMEM((2, 32, 32), jnp.float32),
            pltpu.SMEM((1, 2), jnp.int32),
            pltpu.SemaphoreType.DMA((4,)),
        ],
        compiler_params=small,
    )(phase_delay, attenuation, measured, angles)
    other = lax.ppermute(mine, rows_axis, partner)
    sent = pl.pallas_call(
        pack_measured,
        out_shape=f32(32, 16, 128),
        in_specs=[VMEM] * 3,
        out_specs=HBM,
        scratch_shapes=[
            pltpu.VMEM((512, 128), jnp.float32),
            pltpu.VMEM((32, 16, 128), jnp.float32),
            pltpu.SemaphoreType.DMA((4,)),
        ],
        compiler_params=small,
    )(place, whole, head)
    near = pl.pallas_call(
        pack_sides,
        out_shape=f32(32, 128),
        in_specs=[VMEM] * 3,
        out_specs=VMEM,
        compiler_params=small,
    )(place, mine, other)
    near = lax.ppermute(near, ("illum", "cuts"), beside)
    got = lax.all_to_all(sent, "illum", 0, 0, tiled=True)
    far = lax.ppermute(near, rows_axis, partner)
    across_part, along_part = pl.pallas_call(
        pack_edges,
        out_shape=(f32(3, 8, 128), f32(8, 128)),
        in_specs=[VMEM] * 4,
        out_specs=(VMEM,) * 2,
        compiler_params=small,
    )(place, mine, other, near)
    across_part = lax.ppermute(across_part, rows_axis, across)
    along_part = lax.ppermute(along_part, rows_axis, along)
    here, from_left, from_right = pl.pallas_call(
        pack_rows,
        out_shape=(f32(2, 32, 128), f32(32, 128), f32(32, 128)),
        in_specs=[VMEM] * 7,
        out_specs=(VMEM,) * 3,
        compiler_params=small,
    )(place, mine, other, near, far, across_part, along_part)

    table = pl.pallas_call(
        transmit,
        out_shape=f32(9, 4, 16, 128),
        in_specs=[VMEM] * 4,
        out_specs=VMEM,
        scratch_shapes=[pltpu.VMEM((128, 128), jnp.float32)],
        compiler_params=small,
    )(place, here, from_left, from_right)
    mine, other, edges = pl.pallas_call(
        march,
        out_shape=(f32(32, 128), f32(32, 128), f32(2, 8, 128)),
        in_specs=[VMEM] * 3,
        out_specs=(VMEM,) * 3,
        scratch_shapes=[
            pltpu.VMEM((128, 128), jnp.float32),
            pltpu.VMEM((2, 16, 4, 8, 128), jnp.float32),
            pltpu.VMEM((8, 16, 4, 8, 128), jnp.float32),
            pltpu.VMEM((8, 4, 16, 128), jnp.float32),
        ],
        compiler_params=large,
    )(place, table, got.reshape(512, 128))
    edges = lax.ppermute(edges, rows_axis, across)
    other = pl.pallas_call(
        add_edges,
        out_shape=f32(32, 128),
        in_specs=[VMEM] * 3,
        out_specs=VMEM,
        compiler_params=small,
    )(place, other, edges)
    other = lax.ppermute(other, rows_axis, partner)
    return pl.pallas_call(
        combine,
        out_shape=(f32(2, 32, 32), f32(2, 32, 32)),
        in_specs=[VMEM] * 4,
        out_specs=(VMEM, VMEM),
        compiler_params=small,
    )(place, mine, other, edges)


def solution(mesh):
    placed = (
        P("cuts", "slab", "illum"),
        P("cuts", "slab", "illum"),
        P("illum", None, "slab", None),
        P("illum", None),
    )
    return jax.shard_map(
        body,
        mesh=mesh,
        in_specs=placed,
        out_specs=(P("cuts", "slab", "illum"), P("cuts", "slab", "illum")),
        check_vma=False,
    )
```

```python
import functools
import math

import jax
import jax.numpy as jnp
from jax import lax
from jax.experimental import pallas as pl
from jax.experimental.pallas import tpu as pltpu
from jax.sharding import PartitionSpec as P


step_coeff = 0.08
square_coeff = 0.0032
ratio = step_coeff / square_coeff
two_pi = 2.0 * math.pi

HALO = 8
REACH = 16
VMEM = pl.BlockSpec(memory_space=pltpu.VMEM)
SMEM = pl.BlockSpec(memory_space=pltpu.SMEM)
HBM = pl.BlockSpec(memory_space=pltpu.HBM)
small = pltpu.CompilerParams(vmem_limit_bytes=1 << 20)
large = pltpu.CompilerParams(vmem_limit_bytes=8 << 20)


def f32(*shape):
    return jax.ShapeDtypeStruct(shape, jnp.float32)


def lanes_of(shape):
    return lax.broadcasted_iota(jnp.int32, shape, 1)


def turn(x, by):
    by %= 128
    return pltpu.roll(x, by, 1) if by else x


def pack_object(
    phase_ref, atten_ref, measured_ref, angles_ref,
    out_ref, whole_ref, head_ref,
    phase, atten, turns, sems,
):
    copies = [
        pltpu.make_async_copy(phase_ref, phase, sems.at[0]),
        pltpu.make_async_copy(atten_ref, atten, sems.at[1]),
        pltpu.make_async_copy(angles_ref, turns, sems.at[2]),
        pltpu.make_async_copy(measured_ref.at[0], whole_ref, sems.at[3]),
    ]
    for copy in copies:
        copy.start()
    for copy in copies[:3]:
        copy.wait()
    for n, (ref, layer) in enumerate(((phase, 0), (phase, 1), (atten, 0), (atten, 1))):
        out_ref[:, 32 * n : 32 * n + 32] = ref[layer]
    lane = lanes_of((8, 128))
    head_ref[...] = jnp.where(lane == 0, turns[0, 0], turns[0, 1]).astype(jnp.float32)
    copies[3].wait()


def pairs_of(first, mine_ref, other_ref, rows):
    mine, other = mine_ref[rows], other_ref[rows]
    return [jnp.where(first, mine, other), jnp.where(first, other, mine)]


def sides_of(first, near_ref, far_ref, rows):
    near, far = near_ref[rows], far_ref[rows]
    return [jnp.where(first, near, far), jnp.where(first, far, near)]


def pack_sides(place_ref, mine_ref, other_ref, out_ref):
    first = place_ref[2] == 0
    lane = lanes_of((8, 128))
    spots = 32 * jnp.bitwise_and(lane // 16, 3) + jnp.bitwise_and(lane, 15)
    for block in range(4):
        rows = slice(8 * block, 8 * block + 8)
        both = pairs_of(first, mine_ref, other_ref, rows)
        left, right = (
            jnp.where(lane < 64, *(picked(x, spots + shift) for x in both)) for shift in (0, 16)
        )
        out_ref[rows] = jnp.where(first, left, right)


def pack_edges(place_ref, mine_ref, other_ref, near_ref, far_ref, out_ref):
    first = place_ref[2] == 0
    for n, (of, refs) in enumerate(
        ((pairs_of, (mine_ref, other_ref)), (sides_of, (near_ref, far_ref)))
    ):
        top, bottom = (of(first, *refs, rows) for rows in (slice(0, 8), slice(24, 32)))
        for k in range(2):
            out_ref[2 * n + k] = jnp.where(first, top[k], bottom[k])


def pack_rows(
    place_ref, mine_ref, other_ref, near_ref, far_ref, edge_ref, out_ref, left_ref, right_ref
):
    first = place_ref[2] == 0
    blocks = []
    for block in range(4):
        rows = slice(8 * block, 8 * block + 8)
        blocks.append(
            pairs_of(first, mine_ref, other_ref, rows)
            + sides_of(first, near_ref, far_ref, rows)
        )
    for block in range(4):
        rows = slice(8 * block, 8 * block + 8)
        new = []
        for k in range(4):
            above = blocks[block - 1][k] if block else edge_ref[k]
            below = blocks[block + 1][k] if block < 3 else edge_ref[k]
            new.append(jnp.where(first, above, below))
        out_ref[0, rows], out_ref[1, rows], left_ref[rows], right_ref[rows] = new


def flipped(x):
    rows = 7 - lax.broadcasted_iota(jnp.int32, (8, 128), 0)
    return jnp.take_along_axis(x, rows, axis=0)


def picked(x, lanes):
    return jnp.take_along_axis(x, lanes, axis=1)


def thirds(x):
    parts = []
    for _ in range(3):
        part = x.astype(jnp.bfloat16)
        x = x - part.astype(jnp.float32)
        parts.append(part)
    return jnp.concatenate(parts, axis=1)


def permuted(x, chosen):
    ones = jnp.where(chosen, 1.0, 0.0).astype(jnp.bfloat16)
    return jnp.dot(
        thirds(x),
        jnp.concatenate([ones] * 3, axis=0),
        preferred_element_type=jnp.float32,
    )


def square_iotas(width=128):
    shape = (128, width)
    return lax.broadcasted_iota(jnp.int32, shape, 0), lanes_of(shape)


def pack_measured(place_ref, whole_ref, head_ref, out_ref, plain, packed, sems):
    lane = lanes_of((8, 128))
    head = head_ref[...]
    zero = jnp.zeros((8, 128), jnp.float32)
    source, target = square_iotas()
    m = jnp.bitwise_and(target // 16 - jnp.tile(place_ref[0] // 8, (16, 1)), 3)
    chosen = source == jnp.bitwise_and(target, 64) + 4 * jnp.bitwise_and(target, 15) + m
    cut = place_ref[2]
    regs = []
    for comp in range(2):
        rows = []
        for a in range(2):
            rows.append([])
            for n in range(8):
                at = slice(128 * n, 128 * n + 128)
                x = jnp.where(
                    cut == 0,
                    whole_ref[comp, 8 * a : 8 * a + 8, at],
                    whole_ref[comp, 8 * a + 16 : 8 * a + 24, at],
                )
                rows[a].append(flipped(x) if a else x)
        regs.append(rows)
    copies = []
    for j in range(32):
        v, r = divmod(32 * j - REACH, 128)
        for comp in range(2):
            parts = []
            for a in range(2):
                left = regs[comp][a][v] if v >= 0 else zero
                part = turn(left, 64 * a - r)
                if r > 64:
                    right = regs[comp][a][v + 1] if v + 1 < 8 else zero
                    part = jnp.where(lane - 64 * a < 128 - r, part, turn(right, 64 * a - r))
                parts.append(part)
            both = jnp.where(lane < 64, parts[0], parts[1])
            if comp == 0:
                both = jnp.where(lane < 2, head, both)
            plain[16 * j + 8 * comp : 16 * j + 8 * comp + 8] = both
        if j % 8 == 7:
            part = pl.ds(j - 7, 8)
            moved = permuted(plain[16 * j - 112 : 16 * j + 16], chosen)
            packed[part] = moved.reshape(8, 16, 128)
            copies.append(
                pltpu.make_async_copy(packed.at[part], out_ref.at[part], sems.at[j // 8])
            )
            copies[-1].start()
    for copy in copies:
        copy.wait()


def transmit(place_ref, here_ref, left_ref, right_ref, table, flat):
    sub = lax.broadcasted_iota(jnp.int32, (8, 128), 0)
    block, slab, cut = place_ref[0], place_ref[1], place_ref[2]
    lane = lanes_of((8, 128))
    upper = lane < 64
    window = jnp.bitwise_and(lane, 63)
    place = jnp.bitwise_and(lane, 15)
    top = 32 * slab + 16 * cut - HALO
    left_column = 32 * block - REACH

    def columns(m):
        return left_column + 4 * place + m

    for q in range(2):
        row = top + jnp.where(upper, 8 * q + sub, 31 - 8 * q - sub)
        row_inside = (row >= 0) & (row < 256)
        column = left_column + window
        inside = row_inside & (column >= 0) & (column < 1024)
        for m in range(4):
            column = columns(m)
            table[8, m, 8 * q : 8 * q + 8] = jnp.where(
                row_inside & (column >= 0) & (column < 1024), square_coeff, 0.0
            )
        for layer in range(4):
            pair, sl = divmod(layer, 2)
            values = []
            for n in (sl, 2 + sl):
                halves = []
                for a, b in ((0, q), (1, 3 - q)):
                    rows = slice(8 * b, 8 * b + 8)
                    at = 64 * (a - pair) - 16 * n
                    halves.append(
                        jnp.where(
                            window < 16,
                            turn(left_ref[rows], at),
                            jnp.where(
                                window < 48,
                                turn(here_ref[pair, rows], 64 * a - 32 * n + 16),
                                turn(right_ref[rows], at + 48),
                            ),
                        )
                    )
                values.append(jnp.where(upper, halves[0], flipped(halves[1])))
            damping = jnp.where(inside, jnp.exp(-values[1]), 0.0)
            re, im = damping * jnp.cos(values[0]), damping * jnp.sin(values[0])
            flat[32 * layer + 8 * q : 32 * layer + 8 * q + 8] = re
            flat[32 * layer + 8 * q + 16 : 32 * layer + 8 * q + 24] = im
    source, target = square_iotas(512)
    spot = jnp.bitwise_and(target, 64) + 4 * jnp.bitwise_and(target, 15) + target // 128
    wide = permuted(flat[...], source == spot)
    for m in range(4):
        table[0:8, m] = wide[:, 128 * m : 128 * m + 128].reshape(8, 16, 128)


def march(
    place_ref, table, got_ref,
    mine_ref, other_ref, edge_ref,
    flat, field, stored, sums,
):
    block, slab, cut = place_ref[0], place_ref[1], place_ref[2]
    first = cut == 0
    lane = lanes_of((8, 128))
    upper = lane < 64
    window = jnp.bitwise_and(lane, 63)
    half = jnp.bitwise_and(lane, 64)
    place = jnp.bitwise_and(lane, 15)
    group = jnp.bitwise_and(lane // 16, 3)
    top = 32 * slab + 16 * cut - HALO
    left_column = 32 * block - REACH

    def columns(m):
        return left_column + 4 * place + m

    def spread(n, m, r):
        return jnp.broadcast_to(table[n, m, r : r + 1], (8, 128))

    def side(x, m):
        before = x[m - 1] if m else turn(x[3], 1)
        after = x[m + 1] if m < 3 else turn(x[0], 127)
        return before + after

    def diffract(source, begin, inner, orient, emit):
        rows, scaled = {}, {}

        def around(values, r, k, m):
            parts = [values[n][k][m] for n in (r - 1, r + 1) if n in values]
            if r in values:
                parts.append(side(values[r][k], m))
            return functools.reduce(lambda x, y: x + y, parts)

        def scale(r):
            out = []
            for k in range(2):
                new = []
                for m in range(4):
                    total = around(rows, r, k, m)
                    if r in rows:
                        total = total - 4.0 * rows[r][k][m]
                    new.append(spread(8, m, r) * total)
                out.append(new)
            scaled[r] = out

        def finish(r):
            for m in range(4):
                re, im = (around(scaled, r, k, m) for k in range(2))
                if r in rows:
                    re, im = rows[r][0][m] - re, rows[r][1][m] - im
                else:
                    re, im = -re, -im
                if r in scaled:
                    mre, mim = scaled[r][0][m], scaled[r][1][m]
                    turned = orient * ratio
                    re = re + (4.0 * mre - turned * mim)
                    im = im + (4.0 * mim + turned * mre)
                emit(r, m, re, im)

        def advance(r):
            if r - 1 >= begin + inner:
                scale(r - 1)
            if r - 2 >= begin + 2 * inner:
                finish(r - 2)

        def opposite(row):
            return [[turn(x, 64) for x in part] for part in row]

        for r in range(begin, 16):
            rows[r] = source(r)
            advance(r)
        rows[16] = opposite(rows[15])
        advance(16)
        scaled[16] = opposite(scaled[15])
        finish(15)

    def received(comp, k):
        parts = [
            got_ref[pl.ds(128 * n + 8 * comp + k, 8, stride=16), :] for n in range(4)
        ]
        out = []
        for m in range(4):
            x = parts[3]
            for n in range(3):
                x = jnp.where(group == (m + n) % 4, parts[n], x)
            if m:
                x = picked(x, half + 16 * jnp.bitwise_and(group + m, 3) + place)
            out.append(x)
        return out

    head = received(0, 0)
    corner = jnp.bitwise_and(lane, 48)
    row_turns = picked(head[0], corner)
    col_turns = picked(head[1], corner)
    row0 = (top + jnp.where(upper, 0, 31)).astype(jnp.float32)
    row_part = row_turns * row0 * (1.0 / 256.0)
    col_part = col_turns * columns(0).astype(jnp.float32) * (1.0 / 1024.0)
    row_part = row_part - jnp.floor(row_part)
    col_part = col_part - jnp.floor(col_part)

    def unit(t):
        return jnp.cos(t), jnp.sin(t)

    def times(a, b):
        return a[0] * b[0] - a[1] * b[1], a[0] * b[1] + a[1] * b[0]

    wave = [unit(two_pi * (row_part + col_part))]
    step = unit(two_pi / 256.0 * row_turns * jnp.where(upper, 1.0, -1.0))
    across = unit(two_pi / 1024.0 * col_turns)
    for _ in range(3):
        wave.append(times(wave[-1], across))
    waves = [wave]

    def from_wave(r):
        while len(waves) <= r:
            waves.append([times(x, step) for x in waves[-1]])
        return [[x[k] for x in waves[r]] for k in range(2)]

    def from_field(r):
        return [[field[k, r, m] for m in range(4)] for k in range(2)]

    def forward(layer):
        def source(r):
            re, im = from_wave(r) if layer == 0 else from_field(r)
            out = ([], [])
            for m in range(4):
                v = times((spread(2 * layer, m, r), spread(2 * layer + 1, m, r)), (re[m], im[m]))
                for k in range(2):
                    stored[2 * layer + k, r, m] = v[k]
                    out[k].append(v[k])
            return out

        measured_rows = {}

        def emit(r, m, re, im):
            if layer < 3:
                field[0, r, m], field[1, r, m] = re, im
                return
            if r not in measured_rows:
                measured_rows[r] = [received(k, r - 8) for k in range(2)]
            column = columns(m)
            keep = (column >= 0) & (column < 1024)
            field[0, r, m] = jnp.where(keep, re - measured_rows[r][0][m], 0.0)
            field[1, r, m] = jnp.where(keep, im - measured_rows[r][1][m], 0.0)

        diffract(source, 2 * layer, 1, 1.0, emit)

    def backward(layer):
        def emit(r, m, re, im):
            vre, vim = stored[2 * layer, r, m], stored[2 * layer + 1, r, m]
            for out, x in enumerate((vre * im - vim * re, vre * re + vim * im)):
                sums[2 * layer + out, m, r : r + 1] = jnp.sum(x, axis=0, keepdims=True)
            if layer:
                a, b = spread(2 * layer, m, r), spread(2 * layer + 1, m, r)
                field[0, r, m], field[1, r, m] = a * re + b * im, a * im - b * re

        diffract(from_field, 2 * layer + 2, -1, -1.0, emit)

    for layer in range(4):
        forward(layer)
        for n in range(2):
            for m in range(4):
                if layer:
                    sums[2 * layer + n, m, 0 : 2 * layer] = jnp.zeros((2 * layer, 128))
    for layer in (3, 2, 1, 0):
        backward(layer)

    source, target = square_iotas()
    near = (jnp.bitwise_and(source, 64) == jnp.bitwise_and(target, 64)) & (
        jnp.bitwise_and(source, 15) == jnp.bitwise_and(target, 63) // 4
    )
    total = None
    for m in range(4):
        x = sums[:, m].reshape(128, 128)
        x = permuted(x, near & (jnp.bitwise_and(target, 3) == m))
        total = x if total is None else total + x
    flat[...] = total

    def plain(n, q):
        return flat[16 * n + 8 * q : 16 * n + 8 * q + 8]

    blocks = [[None] * 4 for _ in range(2)]
    for pair in range(2):
        for q in range(2):
            for n in range(4):
                out, sl = divmod(n, 2)
                x = plain(2 * (2 * pair + sl) + out, q)
                x = -x if out else x
                for b, y in ((q, turn(x, 32 * n - 16)), (3 - q, turn(x, 32 * n - 80))):
                    old = blocks[pair][b]
                    blocks[pair][b] = y if old is None else jnp.where(lane < 32 * n, old, y)
        for b in (2, 3):
            blocks[pair][b] = flipped(blocks[pair][b])
    mine = [jnp.where(first, a, b) for a, b in zip(*blocks)]
    other = [jnp.where(first, b, a) for a, b in zip(*blocks)]
    none = jnp.zeros((8, 128), jnp.float32)
    for parts, ref in ((mine, mine_ref), (other, other_ref)):
        for b in range(4):
            ref[8 * b : 8 * b + 8] = jnp.where(
                first, parts[b + 1] if b < 3 else none, parts[b - 1] if b > 0 else none
            )
    for pair in range(2):
        edge_ref[pair] = jnp.where(first, blocks[pair][0], blocks[pair][3])


def add_edges(place_ref, other_ref, edge_ref, out_ref):
    first = place_ref[2] == 0
    edge = jnp.where(first, edge_ref[1], edge_ref[0])
    none = jnp.zeros((8, 128), jnp.float32)
    out_ref[0:8] = other_ref[0:8] + jnp.where(first, edge, none)
    out_ref[8:24] = other_ref[8:24]
    out_ref[24:32] = other_ref[24:32] + jnp.where(first, none, edge)


def combine(place_ref, mine_ref, other_ref, edge_ref, phase_ref, atten_ref):
    first = place_ref[2] == 0
    edge = jnp.where(first, edge_ref[0], edge_ref[1])
    for b in range(4):
        rows = slice(8 * b, 8 * b + 8)
        total = mine_ref[rows] + other_ref[rows]
        if b == 0:
            total = total + jnp.where(first, edge, 0.0)
        if b == 3:
            total = total + jnp.where(first, 0.0, edge)
        for sl in range(2):
            phase_ref[sl, rows] = turn(total, -32 * sl)[:, 0:32]
            atten_ref[sl, rows] = turn(total, -64 - 32 * sl)[:, 0:32]


def body(phase_delay, attenuation, measured, angles):
    block = lax.axis_index("illum")
    slab = lax.axis_index("slab")
    cut = lax.axis_index("cuts")
    place = jnp.stack([jnp.full((8, 128), n, jnp.int32) for n in (block, slab, cut)])
    n_slabs, n_blocks = lax.axis_size("slab"), lax.axis_size("illum")
    rows_axis = ("slab", "cuts")

    def both_ways(pairs):
        return pairs + [(b, a) for a, b in pairs]

    partner = both_ways([(2 * s, 2 * s + 1) for s in range(n_slabs)])
    across = both_ways([(2 * s + 1, 2 * s + 2) for s in range(n_slabs - 1)])
    beside = both_ways([(2 * i + 1, 2 * i + 2) for i in range(n_blocks - 1)])
    phase_delay, attenuation, measured, angles = (
        pltpu.with_memory_space_constraint(x, pltpu.HBM)
        for x in (phase_delay, attenuation, measured, angles)
    )
    mine, whole, head = pl.pallas_call(
        pack_object,
        out_shape=(f32(32, 128), f32(2, 32, 1024), f32(8, 128)),
        in_specs=[HBM] * 4,
        out_specs=(VMEM,) * 3,
        scratch_shapes=[
            pltpu.VMEM((2, 32, 32), jnp.float32),
            pltpu.VMEM((2, 32, 32), jnp.float32),
            pltpu.SMEM((1, 2), jnp.int32),
            pltpu.SemaphoreType.DMA((4,)),
        ],
        compiler_params=small,
    )(phase_delay, attenuation, measured, angles)
    other = lax.ppermute(mine, rows_axis, partner)
    sent = pl.pallas_call(
        pack_measured,
        out_shape=f32(32, 16, 128),
        in_specs=[VMEM] * 3,
        out_specs=HBM,
        scratch_shapes=[
            pltpu.VMEM((512, 128), jnp.float32),
            pltpu.VMEM((32, 16, 128), jnp.float32),
            pltpu.SemaphoreType.DMA((4,)),
        ],
        compiler_params=small,
    )(place, whole, head)
    near = pl.pallas_call(
        pack_sides,
        out_shape=f32(32, 128),
        in_specs=[VMEM] * 3,
        out_specs=VMEM,
        compiler_params=small,
    )(place, mine, other)
    near = lax.ppermute(near, ("illum", "cuts"), beside)
    got = lax.all_to_all(sent, "illum", 0, 0, tiled=True)
    far = lax.ppermute(near, rows_axis, partner)
    edges = pl.pallas_call(
        pack_edges,
        out_shape=f32(4, 8, 128),
        in_specs=[VMEM] * 5,
        out_specs=VMEM,
        compiler_params=small,
    )(place, mine, other, near, far)
    edges = lax.ppermute(edges, rows_axis, across)
    here, from_left, from_right = pl.pallas_call(
        pack_rows,
        out_shape=(f32(2, 32, 128), f32(32, 128), f32(32, 128)),
        in_specs=[VMEM] * 6,
        out_specs=(VMEM,) * 3,
        compiler_params=small,
    )(place, mine, other, near, far, edges)

    table = pl.pallas_call(
        transmit,
        out_shape=f32(9, 4, 16, 128),
        in_specs=[VMEM] * 4,
        out_specs=VMEM,
        scratch_shapes=[pltpu.VMEM((128, 128), jnp.float32)],
        compiler_params=small,
    )(place, here, from_left, from_right)
    mine, other, edges = pl.pallas_call(
        march,
        out_shape=(f32(32, 128), f32(32, 128), f32(2, 8, 128)),
        in_specs=[VMEM] * 3,
        out_specs=(VMEM,) * 3,
        scratch_shapes=[
            pltpu.VMEM((128, 128), jnp.float32),
            pltpu.VMEM((2, 16, 4, 8, 128), jnp.float32),
            pltpu.VMEM((8, 16, 4, 8, 128), jnp.float32),
            pltpu.VMEM((8, 4, 16, 128), jnp.float32),
        ],
        compiler_params=large,
    )(place, table, got.reshape(512, 128))
    edges = lax.ppermute(edges, rows_axis, across)
    other = pl.pallas_call(
        add_edges,
        out_shape=f32(32, 128),
        in_specs=[VMEM] * 3,
        out_specs=VMEM,
        compiler_params=small,
    )(place, other, edges)
    other = lax.ppermute(other, rows_axis, partner)
    return pl.pallas_call(
        combine,
        out_shape=(f32(2, 32, 32), f32(2, 32, 32)),
        in_specs=[VMEM] * 4,
        out_specs=(VMEM, VMEM),
        compiler_params=small,
    )(place, mine, other, edges)


def solution(mesh):
    placed = (
        P("cuts", "slab", "illum"),
        P("cuts", "slab", "illum"),
        P("illum", None, "slab", None),
        P("illum", None),
    )
    return jax.shard_map(
        body,
        mesh=mesh,
        in_specs=placed,
        out_specs=(P("cuts", "slab", "illum"), P("cuts", "slab", "illum")),
        check_vma=False,
    )
```

```python
import functools
import math

import jax
import jax.numpy as jnp
from jax import lax
from jax.experimental import pallas as pl
from jax.experimental.pallas import tpu as pltpu
from jax.sharding import PartitionSpec as P


step_coeff = 0.08
square_coeff = 0.0032
ratio = step_coeff / square_coeff
two_pi = 2.0 * math.pi

HALO = 8
REACH = 16
VMEM = pl.BlockSpec(memory_space=pltpu.VMEM)
SMEM = pl.BlockSpec(memory_space=pltpu.SMEM)
HBM = pl.BlockSpec(memory_space=pltpu.HBM)
small = pltpu.CompilerParams(vmem_limit_bytes=1 << 20)
large = pltpu.CompilerParams(vmem_limit_bytes=8 << 20)


def f32(*shape):
    return jax.ShapeDtypeStruct(shape, jnp.float32)


def lanes_of(shape):
    return lax.broadcasted_iota(jnp.int32, shape, 1)


def turn(x, by):
    by %= 128
    return pltpu.roll(x, by, 1) if by else x


def pack_object(
    phase_ref, atten_ref, measured_ref, angles_ref,
    out_ref, whole_ref, head_ref,
    phase, atten, turns, sems,
):
    copies = [
        pltpu.make_async_copy(phase_ref, phase, sems.at[0]),
        pltpu.make_async_copy(atten_ref, atten, sems.at[1]),
        pltpu.make_async_copy(angles_ref, turns, sems.at[2]),
        pltpu.make_async_copy(measured_ref.at[0], whole_ref, sems.at[3]),
    ]
    for copy in copies:
        copy.start()
    for copy in copies[:3]:
        copy.wait()
    for n, (ref, layer) in enumerate(((phase, 0), (phase, 1), (atten, 0), (atten, 1))):
        out_ref[:, 32 * n : 32 * n + 32] = ref[layer]
    lane = lanes_of((8, 128))
    head_ref[...] = jnp.where(lane == 0, turns[0, 0], turns[0, 1]).astype(jnp.float32)
    copies[3].wait()


def pairs_of(first, mine_ref, other_ref, rows):
    mine, other = mine_ref[rows], other_ref[rows]
    return [jnp.where(first, mine, other), jnp.where(first, other, mine)]


def sides_of(first, near_ref, far_ref, rows):
    near, far = near_ref[rows], far_ref[rows]
    return [jnp.where(first, near, far), jnp.where(first, far, near)]


def pack_sides(place_ref, mine_ref, other_ref, out_ref):
    first = place_ref[2] == 0
    lane = lanes_of((8, 128))
    spots = 32 * jnp.bitwise_and(lane // 16, 3) + jnp.bitwise_and(lane, 15)
    for block in range(4):
        rows = slice(8 * block, 8 * block + 8)
        both = pairs_of(first, mine_ref, other_ref, rows)
        left, right = (
            jnp.where(lane < 64, *(picked(x, spots + shift) for x in both)) for shift in (0, 16)
        )
        out_ref[rows] = jnp.where(first, left, right)


def pack_edges(place_ref, mine_ref, other_ref, near_ref, far_ref, out_ref):
    first = place_ref[2] == 0
    for n, (of, refs) in enumerate(
        ((pairs_of, (mine_ref, other_ref)), (sides_of, (near_ref, far_ref)))
    ):
        top, bottom = (of(first, *refs, rows) for rows in (slice(0, 8), slice(24, 32)))
        for k in range(2):
            out_ref[2 * n + k] = jnp.where(first, top[k], bottom[k])


def pack_rows(
    place_ref, mine_ref, other_ref, near_ref, far_ref, edge_ref, out_ref, left_ref, right_ref
):
    first = place_ref[2] == 0
    blocks = []
    for block in range(4):
        rows = slice(8 * block, 8 * block + 8)
        blocks.append(
            pairs_of(first, mine_ref, other_ref, rows)
            + sides_of(first, near_ref, far_ref, rows)
        )
    for block in range(4):
        rows = slice(8 * block, 8 * block + 8)
        new = []
        for k in range(4):
            above = blocks[block - 1][k] if block else edge_ref[k]
            below = blocks[block + 1][k] if block < 3 else edge_ref[k]
            new.append(jnp.where(first, above, below))
        out_ref[0, rows], out_ref[1, rows], left_ref[rows], right_ref[rows] = new


def flipped(x):
    rows = 7 - lax.broadcasted_iota(jnp.int32, (8, 128), 0)
    return jnp.take_along_axis(x, rows, axis=0)


def picked(x, lanes):
    return jnp.take_along_axis(x, lanes, axis=1)


def thirds(x):
    parts = []
    for _ in range(3):
        part = x.astype(jnp.bfloat16)
        x = x - part.astype(jnp.float32)
        parts.append(part)
    return jnp.concatenate(parts, axis=1)


def permuted(x, chosen):
    ones = jnp.where(chosen, 1.0, 0.0).astype(jnp.bfloat16)
    return jnp.dot(
        thirds(x),
        jnp.concatenate([ones] * 3, axis=0),
        preferred_element_type=jnp.float32,
    )


def square_iotas(width=128):
    shape = (128, width)
    return lax.broadcasted_iota(jnp.int32, shape, 0), lanes_of(shape)


def pack_measured(place_ref, whole_ref, head_ref, out_ref, plain, packed, sems):
    lane = lanes_of((8, 128))
    head = head_ref[...]
    zero = jnp.zeros((8, 128), jnp.float32)
    source, target = square_iotas()
    m = jnp.bitwise_and(target // 16 - jnp.tile(place_ref[0] // 8, (16, 1)), 3)
    chosen = source == jnp.bitwise_and(target, 64) + 4 * jnp.bitwise_and(target, 15) + m
    cut = place_ref[2]
    regs = []
    for comp in range(2):
        rows = []
        for a in range(2):
            rows.append([])
            for n in range(8):
                at = slice(128 * n, 128 * n + 128)
                x = jnp.where(
                    cut == 0,
                    whole_ref[comp, 8 * a : 8 * a + 8, at],
                    whole_ref[comp, 8 * a + 16 : 8 * a + 24, at],
                )
                rows[a].append(flipped(x) if a else x)
        regs.append(rows)
    copies = []
    for j in range(32):
        v, r = divmod(32 * j - REACH, 128)
        for comp in range(2):
            parts = []
            for a in range(2):
                left = regs[comp][a][v] if v >= 0 else zero
                part = turn(left, 64 * a - r)
                if r > 64:
                    right = regs[comp][a][v + 1] if v + 1 < 8 else zero
                    part = jnp.where(lane - 64 * a < 128 - r, part, turn(right, 64 * a - r))
                parts.append(part)
            both = jnp.where(lane < 64, parts[0], parts[1])
            if comp == 0:
                both = jnp.where(lane < 2, head, both)
            plain[16 * j + 8 * comp : 16 * j + 8 * comp + 8] = both
        if j % 8 == 7:
            part = pl.ds(j - 7, 8)
            moved = permuted(plain[16 * j - 112 : 16 * j + 16], chosen)
            packed[part] = moved.reshape(8, 16, 128)
            copies.append(
                pltpu.make_async_copy(packed.at[part], out_ref.at[part], sems.at[j // 8])
            )
            copies[-1].start()
    for copy in copies:
        copy.wait()


def transmit(
    place_ref, mine_ref, other_ref, near_ref, far_ref, edge_ref,
    table, flat, here_ref, left_ref, right_ref,
):
    pack_rows(
        place_ref, mine_ref, other_ref, near_ref, far_ref, edge_ref, here_ref, left_ref, right_ref
    )
    sub = lax.broadcasted_iota(jnp.int32, (8, 128), 0)
    block, slab, cut = place_ref[0], place_ref[1], place_ref[2]
    lane = lanes_of((8, 128))
    upper = lane < 64
    window = jnp.bitwise_and(lane, 63)
    place = jnp.bitwise_and(lane, 15)
    top = 32 * slab + 16 * cut - HALO
    left_column = 32 * block - REACH

    def columns(m):
        return left_column + 4 * place + m

    for q in range(2):
        row = top + jnp.where(upper, 8 * q + sub, 31 - 8 * q - sub)
        row_inside = (row >= 0) & (row < 256)
        column = left_column + window
        inside = row_inside & (column >= 0) & (column < 1024)
        for m in range(4):
            column = columns(m)
            table[8, m, 8 * q : 8 * q + 8] = jnp.where(
                row_inside & (column >= 0) & (column < 1024), square_coeff, 0.0
            )
        for layer in range(4):
            pair, sl = divmod(layer, 2)
            values = []
            for n in (sl, 2 + sl):
                halves = []
                for a, b in ((0, q), (1, 3 - q)):
                    rows = slice(8 * b, 8 * b + 8)
                    at = 64 * (a - pair) - 16 * n
                    halves.append(
                        jnp.where(
                            window < 16,
                            turn(left_ref[rows], at),
                            jnp.where(
                                window < 48,
                                turn(here_ref[pair, rows], 64 * a - 32 * n + 16),
                                turn(right_ref[rows], at + 48),
                            ),
                        )
                    )
                values.append(jnp.where(upper, halves[0], flipped(halves[1])))
            damping = jnp.where(inside, jnp.exp(-values[1]), 0.0)
            re, im = damping * jnp.cos(values[0]), damping * jnp.sin(values[0])
            flat[32 * layer + 8 * q : 32 * layer + 8 * q + 8] = re
            flat[32 * layer + 8 * q + 16 : 32 * layer + 8 * q + 24] = im
    source, target = square_iotas(512)
    spot = jnp.bitwise_and(target, 64) + 4 * jnp.bitwise_and(target, 15) + target // 128
    wide = permuted(flat[...], source == spot)
    for m in range(4):
        table[0:8, m] = wide[:, 128 * m : 128 * m + 128].reshape(8, 16, 128)


def march(
    place_ref, table, got_ref,
    mine_ref, other_ref, edge_ref,
    flat, field, stored, sums,
):
    block, slab, cut = place_ref[0], place_ref[1], place_ref[2]
    first = cut == 0
    lane = lanes_of((8, 128))
    upper = lane < 64
    window = jnp.bitwise_and(lane, 63)
    half = jnp.bitwise_and(lane, 64)
    place = jnp.bitwise_and(lane, 15)
    group = jnp.bitwise_and(lane // 16, 3)
    top = 32 * slab + 16 * cut - HALO
    left_column = 32 * block - REACH

    def columns(m):
        return left_column + 4 * place + m

    def spread(n, m, r):
        return jnp.broadcast_to(table[n, m, r : r + 1], (8, 128))

    def side(x, m):
        before = x[m - 1] if m else turn(x[3], 1)
        after = x[m + 1] if m < 3 else turn(x[0], 127)
        return before + after

    def diffract(source, begin, inner, orient, emit):
        rows, scaled = {}, {}

        def around(values, r, k, m):
            parts = [values[n][k][m] for n in (r - 1, r + 1) if n in values]
            if r in values:
                parts.append(side(values[r][k], m))
            return functools.reduce(lambda x, y: x + y, parts)

        def scale(r):
            out = []
            for k in range(2):
                new = []
                for m in range(4):
                    total = around(rows, r, k, m)
                    if r in rows:
                        total = total - 4.0 * rows[r][k][m]
                    new.append(spread(8, m, r) * total)
                out.append(new)
            scaled[r] = out

        def finish(r):
            for m in range(4):
                re, im = (around(scaled, r, k, m) for k in range(2))
                if r in rows:
                    re, im = rows[r][0][m] - re, rows[r][1][m] - im
                else:
                    re, im = -re, -im
                if r in scaled:
                    mre, mim = scaled[r][0][m], scaled[r][1][m]
                    turned = orient * ratio
                    re = re + (4.0 * mre - turned * mim)
                    im = im + (4.0 * mim + turned * mre)
                emit(r, m, re, im)

        def advance(r):
            if r - 1 >= begin + inner:
                scale(r - 1)
            if r - 2 >= begin + 2 * inner:
                finish(r - 2)

        def opposite(row):
            return [[turn(x, 64) for x in part] for part in row]

        for r in range(begin, 16):
            rows[r] = source(r)
            advance(r)
        rows[16] = opposite(rows[15])
        advance(16)
        scaled[16] = opposite(scaled[15])
        finish(15)

    def received(comp, k):
        parts = [
            got_ref[pl.ds(128 * n + 8 * comp + k, 8, stride=16), :] for n in range(4)
        ]
        out = []
        for m in range(4):
            x = parts[3]
            for n in range(3):
                x = jnp.where(group == (m + n) % 4, parts[n], x)
            if m:
                x = picked(x, half + 16 * jnp.bitwise_and(group + m, 3) + place)
            out.append(x)
        return out

    head = received(0, 0)
    corner = jnp.bitwise_and(lane, 48)
    row_turns = picked(head[0], corner)
    col_turns = picked(head[1], corner)
    row0 = (top + jnp.where(upper, 0, 31)).astype(jnp.float32)
    row_part = row_turns * row0 * (1.0 / 256.0)
    col_part = col_turns * columns(0).astype(jnp.float32) * (1.0 / 1024.0)
    row_part = row_part - jnp.floor(row_part)
    col_part = col_part - jnp.floor(col_part)

    def unit(t):
        return jnp.cos(t), jnp.sin(t)

    def times(a, b):
        return a[0] * b[0] - a[1] * b[1], a[0] * b[1] + a[1] * b[0]

    wave = [unit(two_pi * (row_part + col_part))]
    step = unit(two_pi / 256.0 * row_turns * jnp.where(upper, 1.0, -1.0))
    across = unit(two_pi / 1024.0 * col_turns)
    for _ in range(3):
        wave.append(times(wave[-1], across))
    waves = [wave]

    def from_wave(r):
        while len(waves) <= r:
            waves.append([times(x, step) for x in waves[-1]])
        return [[x[k] for x in waves[r]] for k in range(2)]

    def from_field(r):
        return [[field[k, r, m] for m in range(4)] for k in range(2)]

    def forward(layer):
        def source(r):
            re, im = from_wave(r) if layer == 0 else from_field(r)
            out = ([], [])
            for m in range(4):
                v = times((spread(2 * layer, m, r), spread(2 * layer + 1, m, r)), (re[m], im[m]))
                for k in range(2):
                    stored[2 * layer + k, r, m] = v[k]
                    out[k].append(v[k])
            return out

        measured_rows = {}

        def emit(r, m, re, im):
            if layer < 3:
                field[0, r, m], field[1, r, m] = re, im
                return
            if r not in measured_rows:
                measured_rows[r] = [received(k, r - 8) for k in range(2)]
            column = columns(m)
            keep = (column >= 0) & (column < 1024)
            field[0, r, m] = jnp.where(keep, re - measured_rows[r][0][m], 0.0)
            field[1, r, m] = jnp.where(keep, im - measured_rows[r][1][m], 0.0)

        diffract(source, 2 * layer, 1, 1.0, emit)

    def backward(layer):
        def emit(r, m, re, im):
            vre, vim = stored[2 * layer, r, m], stored[2 * layer + 1, r, m]
            for out, x in enumerate((vre * im - vim * re, vre * re + vim * im)):
                sums[2 * layer + out, m, r : r + 1] = jnp.sum(x, axis=0, keepdims=True)
            if layer:
                a, b = spread(2 * layer, m, r), spread(2 * layer + 1, m, r)
                field[0, r, m], field[1, r, m] = a * re + b * im, a * im - b * re

        diffract(from_field, 2 * layer + 2, -1, -1.0, emit)

    for layer in range(4):
        forward(layer)
        for n in range(2):
            for m in range(4):
                if layer:
                    sums[2 * layer + n, m, 0 : 2 * layer] = jnp.zeros((2 * layer, 128))
    for layer in (3, 2, 1, 0):
        backward(layer)

    source, target = square_iotas()
    near = (jnp.bitwise_and(source, 64) == jnp.bitwise_and(target, 64)) & (
        jnp.bitwise_and(source, 15) == jnp.bitwise_and(target, 63) // 4
    )
    total = None
    for m in range(4):
        x = sums[:, m].reshape(128, 128)
        x = permuted(x, near & (jnp.bitwise_and(target, 3) == m))
        total = x if total is None else total + x
    flat[...] = total

    def plain(n, q):
        return flat[16 * n + 8 * q : 16 * n + 8 * q + 8]

    blocks = [[None] * 4 for _ in range(2)]
    for pair in range(2):
        for q in range(2):
            for n in range(4):
                out, sl = divmod(n, 2)
                x = plain(2 * (2 * pair + sl) + out, q)
                x = -x if out else x
                for b, y in ((q, turn(x, 32 * n - 16)), (3 - q, turn(x, 32 * n - 80))):
                    old = blocks[pair][b]
                    blocks[pair][b] = y if old is None else jnp.where(lane < 32 * n, old, y)
        for b in (2, 3):
            blocks[pair][b] = flipped(blocks[pair][b])
    mine = [jnp.where(first, a, b) for a, b in zip(*blocks)]
    other = [jnp.where(first, b, a) for a, b in zip(*blocks)]
    none = jnp.zeros((8, 128), jnp.float32)
    for parts, ref in ((mine, mine_ref), (other, other_ref)):
        for b in range(4):
            ref[8 * b : 8 * b + 8] = jnp.where(
                first, parts[b + 1] if b < 3 else none, parts[b - 1] if b > 0 else none
            )
    for pair in range(2):
        edge_ref[pair] = jnp.where(first, blocks[pair][0], blocks[pair][3])


def add_edges(place_ref, other_ref, edge_ref, out_ref):
    first = place_ref[2] == 0
    edge = jnp.where(first, edge_ref[1], edge_ref[0])
    none = jnp.zeros((8, 128), jnp.float32)
    out_ref[0:8] = other_ref[0:8] + jnp.where(first, edge, none)
    out_ref[8:24] = other_ref[8:24]
    out_ref[24:32] = other_ref[24:32] + jnp.where(first, none, edge)


def combine(place_ref, mine_ref, other_ref, edge_ref, phase_ref, atten_ref):
    first = place_ref[2] == 0
    edge = jnp.where(first, edge_ref[0], edge_ref[1])
    for b in range(4):
        rows = slice(8 * b, 8 * b + 8)
        total = mine_ref[rows] + other_ref[rows]
        if b == 0:
            total = total + jnp.where(first, edge, 0.0)
        if b == 3:
            total = total + jnp.where(first, 0.0, edge)
        for sl in range(2):
            phase_ref[sl, rows] = turn(total, -32 * sl)[:, 0:32]
            atten_ref[sl, rows] = turn(total, -64 - 32 * sl)[:, 0:32]


def body(phase_delay, attenuation, measured, angles):
    block = lax.axis_index("illum")
    slab = lax.axis_index("slab")
    cut = lax.axis_index("cuts")
    place = jnp.stack([jnp.full((8, 128), n, jnp.int32) for n in (block, slab, cut)])
    n_slabs, n_blocks = lax.axis_size("slab"), lax.axis_size("illum")
    rows_axis = ("slab", "cuts")

    def both_ways(pairs):
        return pairs + [(b, a) for a, b in pairs]

    partner = both_ways([(2 * s, 2 * s + 1) for s in range(n_slabs)])
    across = both_ways([(2 * s + 1, 2 * s + 2) for s in range(n_slabs - 1)])
    beside = both_ways([(2 * i + 1, 2 * i + 2) for i in range(n_blocks - 1)])
    phase_delay, attenuation, measured, angles = (
        pltpu.with_memory_space_constraint(x, pltpu.HBM)
        for x in (phase_delay, attenuation, measured, angles)
    )
    mine, whole, head = pl.pallas_call(
        pack_object,
        out_shape=(f32(32, 128), f32(2, 32, 1024), f32(8, 128)),
        in_specs=[HBM] * 4,
        out_specs=(VMEM,) * 3,
        scratch_shapes=[
            pltpu.VMEM((2, 32, 32), jnp.float32),
            pltpu.VMEM((2, 32, 32), jnp.float32),
            pltpu.SMEM((1, 2), jnp.int32),
            pltpu.SemaphoreType.DMA((4,)),
        ],
        compiler_params=small,
    )(phase_delay, attenuation, measured, angles)
    other = lax.ppermute(mine, rows_axis, partner)
    sent = pl.pallas_call(
        pack_measured,
        out_shape=f32(32, 16, 128),
        in_specs=[VMEM] * 3,
        out_specs=HBM,
        scratch_shapes=[
            pltpu.VMEM((512, 128), jnp.float32),
            pltpu.VMEM((32, 16, 128), jnp.float32),
            pltpu.SemaphoreType.DMA((4,)),
        ],
        compiler_params=small,
    )(place, whole, head)
    near = pl.pallas_call(
        pack_sides,
        out_shape=f32(32, 128),
        in_specs=[VMEM] * 3,
        out_specs=VMEM,
        compiler_params=small,
    )(place, mine, other)
    near = lax.ppermute(near, ("illum", "cuts"), beside)
    got = lax.all_to_all(sent, "illum", 0, 0, tiled=True)
    far = lax.ppermute(near, rows_axis, partner)
    edges = pl.pallas_call(
        pack_edges,
        out_shape=f32(4, 8, 128),
        in_specs=[VMEM] * 5,
        out_specs=VMEM,
        compiler_params=small,
    )(place, mine, other, near, far)
    edges = lax.ppermute(edges, rows_axis, across)
    table = pl.pallas_call(
        transmit,
        out_shape=f32(9, 4, 16, 128),
        in_specs=[VMEM] * 6,
        out_specs=VMEM,
        scratch_shapes=[
            pltpu.VMEM((128, 128), jnp.float32),
            pltpu.VMEM((2, 32, 128), jnp.float32),
            pltpu.VMEM((32, 128), jnp.float32),
            pltpu.VMEM((32, 128), jnp.float32),
        ],
        compiler_params=small,
    )(place, mine, other, near, far, edges)
    mine, other, edges = pl.pallas_call(
        march,
        out_shape=(f32(32, 128), f32(32, 128), f32(2, 8, 128)),
        in_specs=[VMEM] * 3,
        out_specs=(VMEM,) * 3,
        scratch_shapes=[
            pltpu.VMEM((128, 128), jnp.float32),
            pltpu.VMEM((2, 16, 4, 8, 128), jnp.float32),
            pltpu.VMEM((8, 16, 4, 8, 128), jnp.float32),
            pltpu.VMEM((8, 4, 16, 128), jnp.float32),
        ],
        compiler_params=large,
    )(place, table, got.reshape(512, 128))
    edges = lax.ppermute(edges, rows_axis, across)
    other = pl.pallas_call(
        add_edges,
        out_shape=f32(32, 128),
        in_specs=[VMEM] * 3,
        out_specs=VMEM,
        compiler_params=small,
    )(place, other, edges)
    other = lax.ppermute(other, rows_axis, partner)
    return pl.pallas_call(
        combine,
        out_shape=(f32(2, 32, 32), f32(2, 32, 32)),
        in_specs=[VMEM] * 4,
        out_specs=(VMEM, VMEM),
        compiler_params=small,
    )(place, mine, other, edges)


def solution(mesh):
    placed = (
        P("cuts", "slab", "illum"),
        P("cuts", "slab", "illum"),
        P("illum", None, "slab", None),
        P("illum", None),
    )
    return jax.shard_map(
        body,
        mesh=mesh,
        in_specs=placed,
        out_specs=(P("cuts", "slab", "illum"), P("cuts", "slab", "illum")),
        check_vma=False,
    )
```
